256 devices in a mesh: seq: 32 (over z, x), val: 8 (over y, core).
Axes of the slice: x: 4, y: 4, z: 8, core: 2. Of those that a mesh axis runs over, the one named last changes fastest.
Arguments:
- queries: bfloat16 [16, 16, 32768], P('val', None, 'seq'), may hold values from -8 to 8
- keys: bfloat16 [16, 16, 32768], P('val', None, 'seq'), may hold values from -8 to 8
- values: bfloat16 [16, 128, 32768], P(None, 'val', 'seq'), may hold values from -4 to 4
- out_grad: bfloat16 [16, 128, 32768], P(None, 'val', 'seq'), may hold values from -4 to 4
Outputs:
- mixed: bfloat16 [16, 128, 32768], P(None, 'val', 'seq')
- query_grad: float32 [16, 16, 32768], P('val', None, 'seq')
- key_grad: float32 [16, 16, 32768], P('val', None, 'seq')
- value_grad: bfloat16 [16, 128, 32768], P(None, 'val', 'seq')
The draws below stay inside these ranges and needn't reach their ends.
All inputs are finite; a program needn't handle non-finite values.
Results may differ from the reference program's by a relative error of at most 0.019.
Values may be sent and summed in bfloat16 or wider, within the bound.
A program may use at most 128 MiB of HBM per device.

```python
import math
import jax
import jax.numpy as jnp
from jax import lax

H = 16
HK = 16
EV = 128
W = 512
TOKENS = 32768


def draw_pair(seed_key):
    folded = jax.random.fold_in(seed_key, 7)
    query_key, other_key, query_scale_key, key_scale_key = jax.random.split(folded, 4)
    array_shape = (H, HK, TOKENS)
    query_jitter = jax.random.normal(query_key, array_shape, jnp.float32)
    key_jitter = jax.random.normal(other_key, array_shape, jnp.float32)
    lowest = 0.4
    query_scale = jnp.exp(jax.random.uniform(query_scale_key, (H, 1, TOKENS), jnp.float32, math.log(lowest), math.log(4.0)))
    key_scale = jnp.exp(jax.random.uniform(key_scale_key, (H, 1, TOKENS), jnp.float32, math.log(lowest), math.log(4.0)))
    query_out = jnp.clip(query_jitter * query_scale, -8.0, 8.0)
    key_out = jnp.clip(key_jitter * key_scale, -8.0, 8.0)
    return (query_out, key_out)


def wave_draw(seed_key, salt, partner_rows):
    folded = jax.random.fold_in(seed_key, salt)
    jitter_key, freq_key, phase_key, amp_key = jax.random.split(folded, 4)
    array_shape = (H, EV, TOKENS)
    frequency = jax.random.uniform(freq_key, (H, EV, 1), jnp.float32, 0.5, 2.0)
    phases = jax.random.uniform(phase_key, (H, EV, 1), jnp.float32, -math.pi, math.pi)
    amplitude = jax.random.uniform(amp_key, (H, EV, 1), jnp.float32, 0.5, 1.5)
    positions = lax.broadcasted_iota(jnp.float32, (1, 1, TOKENS), 2) / TOKENS
    waveform = jnp.sin(2.0 * math.pi * frequency * positions + phases)
    jitter = 0.8 * jax.random.normal(jitter_key, array_shape, jnp.float32)
    channel_map = lax.broadcasted_iota(jnp.int32, (EV,), 0) % HK
    partner = jnp.take(partner_rows, channel_map, axis=1)
    return jnp.clip(jitter + amplitude * waveform + 0.8 * partner, -4.0, 4.0).astype(jnp.bfloat16)


def draw_queries(key, part):
    return draw_pair(key)[0].astype(jnp.bfloat16)


def draw_keys(key, part):
    return draw_pair(key)[1].astype(jnp.bfloat16)


def draw_values(key, part):
    return wave_draw(key, 21, draw_pair(key)[1])


def draw_out_grad(key, part):
    return wave_draw(key, 33, draw_pair(key)[0])


def setup_inputs(seed: int = 0) -> dict:
    key_of = jax.random.split(jax.random.key(seed), 5)
    queries = draw_queries(jax.random.fold_in(key_of[4], 71), 0)
    keys = draw_keys(jax.random.fold_in(key_of[4], 71), 0)
    values = draw_values(jax.random.fold_in(key_of[4], 71), 0)
    out_grad = draw_out_grad(jax.random.fold_in(key_of[4], 71), 0)
    return dict(queries=queries, keys=keys, values=values, out_grad=out_grad)


ROOT_HALF = 0.7071067811865476
NEG_LARGE = -1e+30
PRECISE = lax.Precision.HIGHEST

def rounded(array_in):
    return lax.optimization_barrier(array_in.astype(jnp.bfloat16)).astype(jnp.float32)

def features(rows_in):
    key_width = rows_in.shape[-2]
    scaled = rows_in.astype(jnp.float32) * key_width ** (-0.25)
    products = scaled[..., :, None, :] * scaled[..., None, :, :] * ROOT_HALF
    leading = scaled.shape[:-2]
    length = scaled.shape[-1]
    ones_row = jnp.ones(leading + (1, length), jnp.float32)
    quadratic = products.reshape(leading + (key_width * key_width, length))
    return jnp.concatenate([ones_row, scaled, quadratic], axis=-2).astype(jnp.bfloat16)

def feature_grad(feat_grad, rows_in):
    key_width = rows_in.shape[-2]
    factor = key_width ** (-0.25)
    scaled = rows_in.astype(jnp.float32) * factor
    leading = scaled.shape[:-2]
    length = scaled.shape[-1]
    quadratic = feat_grad[..., 1 + key_width:, :].reshape(leading + (key_width, key_width, length))
    symmetric = quadratic + jnp.swapaxes(quadratic, -3, -2)
    folded = jnp.einsum('...abt,...bt->...at', symmetric, scaled, precision=PRECISE)
    return factor * (feat_grad[..., 1:1 + key_width, :] + ROOT_HALF * folded)

def window_masks(span_len, prev_ok):
    row_ids = lax.broadcasted_iota(jnp.int32, (span_len, span_len), 0)
    col_ids = lax.broadcasted_iota(jnp.int32, (span_len, span_len), 1)
    return (col_ids <= row_ids, jnp.logical_and(col_ids > row_ids, prev_ok))

def scores_of(query_blk, key_own, key_prev):
    scaling = query_blk.shape[-2] ** (-0.5)
    query_wide = query_blk.astype(jnp.float32)
    own_scores = jnp.einsum('...ct,...cj->...tj', query_wide, key_own.astype(jnp.float32), precision=PRECISE) * scaling
    prev_scores = jnp.einsum('...ct,...cj->...tj', query_wide, key_prev.astype(jnp.float32), precision=PRECISE) * scaling
    return (own_scores, prev_scores)

def soft_weights(own_scores, prev_scores, own_mask, prev_mask, log_total):
    own_soft = jnp.where(own_mask, jnp.exp(own_scores - log_total[..., :, None]), 0.0)
    prev_soft = jnp.where(prev_mask, jnp.exp(prev_scores - log_total[..., :, None]), 0.0)
    return (rounded(own_soft), rounded(prev_soft))

def local_forward(query_blk, key_own, key_prev, value_own, value_prev, prev_ok):
    own_scores, prev_scores = scores_of(query_blk, key_own, key_prev)
    own_mask, prev_mask = window_masks(own_scores.shape[-1], prev_ok)
    taylor = jnp.where(own_mask, 1.0 + own_scores + 0.5 * own_scores * own_scores, 0.0)
    den_intra = lax.optimization_barrier(jnp.sum(taylor, axis=-1))
    value_wide = value_own.astype(jnp.float32)
    prev_wide = value_prev.astype(jnp.float32)
    num_intra = jnp.einsum('...tj,...ej->...et', rounded(taylor), value_wide, precision=PRECISE)
    row_top = jnp.maximum(lax.optimization_barrier(jnp.max(jnp.where(own_mask, own_scores, NEG_LARGE), axis=-1)), lax.optimization_barrier(jnp.max(jnp.where(prev_mask, prev_scores, NEG_LARGE), axis=-1)))
    totals = lax.optimization_barrier(jnp.sum(jnp.where(own_mask, jnp.exp(own_scores - row_top[..., None]), 0.0), axis=-1))
    totals = totals + lax.optimization_barrier(jnp.sum(jnp.where(prev_mask, jnp.exp(prev_scores - row_top[..., None]), 0.0), axis=-1))
    log_total = row_top + jnp.log(totals)
    own_soft, prev_soft = soft_weights(own_scores, prev_scores, own_mask, prev_mask, log_total)
    window_out = jnp.einsum('...tj,...ej->...et', own_soft, value_wide, precision=PRECISE)
    window_out = window_out + jnp.einsum('...tj,...ej->...et', prev_soft, prev_wide, precision=PRECISE)
    return (num_intra, den_intra, window_out, log_total)

def local_backward(query_blk, key_own, key_prev, value_own, value_prev, prev_ok, grad_blk, dn_wide, dd_row, delta_row, log_total):
    own_scores, prev_scores = scores_of(query_blk, key_own, key_prev)
    own_mask, prev_mask = window_masks(own_scores.shape[-1], prev_ok)
    taylor_low = rounded(jnp.where(own_mask, 1.0 + own_scores + 0.5 * own_scores * own_scores, 0.0))
    own_soft, prev_soft = soft_weights(own_scores, prev_scores, own_mask, prev_mask, log_total)
    grad_wide = grad_blk.astype(jnp.float32)
    value_wide = value_own.astype(jnp.float32)
    prev_wide = value_prev.astype(jnp.float32)
    mixing = jnp.einsum('...et,...ej->...tj', dn_wide, value_wide, precision=PRECISE) + dd_row[..., :, None]
    taylor_part = jnp.where(own_mask, mixing * (1.0 + own_scores), 0.0)
    own_grad = taylor_part + own_soft * (jnp.einsum('...et,...ej->...tj', grad_wide, value_wide, precision=PRECISE) - delta_row[..., :, None])
    prev_grad = prev_soft * (jnp.einsum('...et,...ej->...tj', grad_wide, prev_wide, precision=PRECISE) - delta_row[..., :, None])
    scaling = query_blk.shape[-2] ** (-0.5)
    query_wide = query_blk.astype(jnp.float32)
    query_part = jnp.einsum('...tj,...cj->...ct', own_grad, key_own.astype(jnp.float32), precision=PRECISE)
    query_part = scaling * (query_part + jnp.einsum('...tj,...cj->...ct', prev_grad, key_prev.astype(jnp.float32), precision=PRECISE))
    key_part = scaling * jnp.einsum('...tj,...ct->...cj', own_grad, query_wide, precision=PRECISE)
    key_prev_part = scaling * jnp.einsum('...tj,...ct->...cj', prev_grad, query_wide, precision=PRECISE)
    value_part = jnp.einsum('...tj,...et->...ej', taylor_low, dn_wide, precision=PRECISE)
    value_part = value_part + jnp.einsum('...tj,...et->...ej', own_soft, grad_wide, precision=PRECISE)
    value_prev_part = jnp.einsum('...tj,...et->...ej', prev_soft, grad_wide, precision=PRECISE)
    return (query_part, key_part, value_part, key_prev_part, value_prev_part)

def reference(queries, keys, values, out_grad):
    head_count, key_width, length = queries.shape
    channels = values.shape[1]
    blocks = length // W
    feat_count = 1 + key_width + key_width * key_width

    def split_blocks(array_in):
        return jnp.moveaxis(array_in.reshape(array_in.shape[0], array_in.shape[1], blocks, W), 2, 0)

    def previous(blocked):
        return jnp.concatenate([jnp.zeros_like(blocked[:1]), blocked[:-1]], axis=0)

    def join_blocks(blocked):
        return jnp.moveaxis(blocked, 0, 2).reshape(blocked.shape[1], blocked.shape[2], length)
    query_blocks = split_blocks(queries)
    key_blocks = split_blocks(keys)
    value_blocks = split_blocks(values)
    grad_blocks = split_blocks(out_grad)
    key_before = previous(key_blocks)
    value_before = previous(value_blocks)
    has_before = jnp.arange(blocks) > 0

    def forward_step(carried, sliced):
        lin_state, norm_state = carried
        query_blk, key_own, key_prev, value_own, value_prev, prev_ok = sliced
        query_feat = features(query_blk).astype(jnp.float32)
        key_feat = features(key_own).astype(jnp.float32)
        num_intra, den_intra, window_out, log_total = local_forward(query_blk, key_own, key_prev, value_own, value_prev, prev_ok)
        denominator = den_intra + jnp.einsum('hft,hf->ht', query_feat, norm_state, precision=PRECISE)
        numerator = num_intra + jnp.einsum('hft,hfe->het', query_feat, lin_state, precision=PRECISE)
        linear_out = numerator / denominator[:, None, :]
        mixed_blk = (linear_out + window_out).astype(jnp.bfloat16)
        new_state = lin_state + jnp.einsum('hfj,hej->hfe', key_feat, value_own.astype(jnp.float32), precision=PRECISE)
        new_norm = norm_state + lax.optimization_barrier(jnp.sum(key_feat, axis=-1))
        return ((new_state, new_norm), (mixed_blk, linear_out, window_out, denominator, log_total, lin_state, norm_state))
    start_state = (jnp.zeros((head_count, feat_count, channels), jnp.float32), jnp.zeros((head_count, feat_count), jnp.float32))
    unused, saved = lax.scan(forward_step, start_state, (query_blocks, key_blocks, key_before, value_blocks, value_before, has_before))
    mixed_blocks, linear_blocks, window_blocks, denom_blocks, log_blocks, state_blocks, norm_blocks = saved

    def backward_step(carried, sliced):
        suffix, dd_suffix, carried_key, carried_value = carried
        query_blk, key_own, key_prev, value_own, value_prev, prev_ok, grad_blk, linear_out, window_out, denominator, log_total, lin_state, norm_state = sliced
        grad_wide = grad_blk.astype(jnp.float32)
        dn_wide = rounded(grad_wide / denominator[:, None, :])
        dd_row = -lax.optimization_barrier(jnp.sum(grad_wide * linear_out, axis=1)) / denominator
        delta_row = lax.optimization_barrier(jnp.sum(grad_wide * window_out, axis=1))
        query_part, key_part, value_part, key_prev_part, value_prev_part = local_backward(query_blk, key_own, key_prev, value_own, value_prev, prev_ok, grad_blk, dn_wide, dd_row, delta_row, log_total)
        query_feat = features(query_blk).astype(jnp.float32)
        key_feat = features(key_own).astype(jnp.float32)
        query_feat_grad = jnp.einsum('hfe,het->hft', lin_state, dn_wide, precision=PRECISE) + norm_state[:, :, None] * dd_row[:, None, :]
        key_feat_grad = jnp.einsum('hfe,hej->hfj', suffix, value_own.astype(jnp.float32), precision=PRECISE) + dd_suffix[:, :, None]
        value_inter = jnp.einsum('hfj,hfe->hej', key_feat, suffix, precision=PRECISE)
        query_grad_blk = query_part + feature_grad(query_feat_grad, query_blk)
        key_grad_blk = key_part + carried_key + feature_grad(key_feat_grad, key_own)
        value_grad_blk = (value_part + carried_value + value_inter).astype(jnp.bfloat16)
        new_suffix = suffix + jnp.einsum('hft,het->hfe', query_feat, dn_wide, precision=PRECISE)
        new_dd = dd_suffix + jnp.einsum('hft,ht->hf', query_feat, dd_row, precision=PRECISE)
        return ((new_suffix, new_dd, key_prev_part, value_prev_part), (query_grad_blk, key_grad_blk, value_grad_blk))
    start_grad = (jnp.zeros((head_count, feat_count, channels), jnp.float32), jnp.zeros((head_count, feat_count), jnp.float32), jnp.zeros((head_count, key_width, W), jnp.float32), jnp.zeros((head_count, channels, W), jnp.float32))
    unused_grad, grads = lax.scan(backward_step, start_grad, (query_blocks, key_blocks, key_before, value_blocks, value_before, has_before, grad_blocks, linear_blocks, window_blocks, denom_blocks, log_blocks, state_blocks, norm_blocks), reverse=True)
    query_grad_blocks, key_grad_blocks, value_grad_blocks = grads
    return (join_blocks(mixed_blocks), join_blocks(query_grad_blocks), join_blocks(key_grad_blocks), join_blocks(value_grad_blocks))
```

```python
import functools

import jax
import jax.numpy as jnp
from jax import lax
from jax.experimental import pallas as pl
from jax.experimental.pallas import tpu as pltpu
from jax.sharding import PartitionSpec as P

W = 512
CH = 256
NX = 4
FR = 192
QR = FR // NX
LIN = 144
ROOT_HALF = 0.7071067811865476
NEG_LARGE = -1e30
MESH = pl.DeviceIdType.MESH
F32 = jnp.float32
BF16 = jnp.bfloat16


def dot(a, b, ca, cb):
    return lax.dot_general(a, b, (((ca,), (cb,)), ((), ())), preferred_element_type=F32)


def nn(a, b):
    return dot(a, b, 1, 0)


def nt(a, b):
    return dot(a, b, 1, 1)


def tn(a, b):
    return dot(a, b, 0, 0)


def turn_up(x, d):
    return jnp.concatenate([x[d:], x[:d]], axis=0) if d else x


def turn_down(x, d):
    return turn_up(x, 16 - d)


def split_rows(row):
    high = row.astype(BF16).astype(F32)
    low = row - high
    index = lax.broadcasted_iota(jnp.int32, (16, row.shape[1]), 0)
    return jnp.where(index == 0, high, jnp.where(index == 1, low, 0.0)).astype(BF16)


def pair_weights(columns):
    row = lax.broadcasted_iota(jnp.int32, (FR, columns), 0)
    return jnp.where(jnp.logical_and(row >= 16, row < 128), 2.0, 1.0)


def kernel(
    n_seq,
    n_val,
    q_ref,
    k_ref,
    v_hbm,
    g_hbm,
    mixed_out,
    dq_out,
    dk_out,
    dv_out,
    kx,
    vx,
    vt,
    gx,
    fq,
    fk,
    es,
    cs,
    ts,
    num,
    win,
    kc,
    deni,
    rden,
    dd,
    dl,
    dn,
    dqa,
    dka,
    dva,
    mix,
    dvb,
    nrow,
    nsend,
    nxbuf,
    ntot,
    nzbuf,
    npre,
    ncol,
    drow,
    dsend,
    dxbuf,
    dtot,
    dzbuf,
    dsuf,
    s_blk,
    s_send,
    s_x,
    s_tot,
    s_z,
    s_acc,
    s_out,
    s_pre,
    u_blk,
    u_send,
    u_x,
    u_tot,
    u_z,
    u_acc,
    u_out,
    u_pre,
    hk_send,
    hv_send,
    hk_recv,
    hv_recv,
    va_s,
    va_r,
    ga_s,
    ga_r,
    mo_s,
    mo_r,
    do_s,
    do_r,
    loc,
    kh,
    vh,
    gkh,
    gvh,
    nxs,
    nxr,
    nzs,
    nzr,
    dxs,
    dxr,
    dzs,
    dzr,
    sxs,
    sxr,
    szs,
    szr,
    sos,
    sor,
    uxs,
    uxr,
    uzs,
    uzr,
    uos,
    uor,
):
    heads = q_ref.shape[0]
    tokens = q_ref.shape[2]
    blocks = tokens // W
    part = v_hbm.shape[1]
    nz = n_seq // NX
    seq = lax.axis_index("seq")
    val = lax.axis_index("val")
    z = seq // NX
    x = lax.rem(seq, NX)
    first = seq == 0
    last = seq == n_seq - 1
    after = lax.rem(seq + 1, n_seq)
    ahead = lax.rem(seq + n_seq - 1, n_seq)

    def remote(src, dst, ssem, rsem, s, v):
        return pltpu.make_async_remote_copy(
            src_ref=src, dst_ref=dst, send_sem=ssem, recv_sem=rsem, device_id=(s, v), device_id_type=MESH
        )

    def val_peer(d):
        return lax.rem(val + d, n_val)

    def x_peer(d):
        return z * NX + lax.rem(x + d, NX)

    barrier = pltpu.get_barrier_semaphore()

    def greet(s, v):
        pl.semaphore_signal(barrier, inc=1, device_id=(s, v), device_id_type=MESH)

    for d in range(1, n_val):
        greet(seq, val_peer(d))
    for d in range(1, NX):
        greet(x_peer(d), val)
    for d in range(1, nz):
        greet(lax.rem(z + d, nz) * NX + x, val)
    greet(after, val)
    greet(ahead, val)

    kx[:, :, W:] = k_ref[...]

    @pl.when(first)
    def _():
        kx[:, :, :W] = jnp.zeros((heads, 16, W), BF16)
        vx[:, :, :W] = jnp.zeros((heads, 128, W), BF16)

    pl.semaphore_wait(barrier, (n_val - 1) + (NX - 1) + (nz - 1) + 2)

    mine = pl.ds(pl.multiple_of(val * part, part), part)

    def gather_copy(src, dst, off, ssem, rsem, d):
        peer = val_peer(d)
        return remote(
            src.at[pl.ds(peer * heads, heads)], dst.at[:, mine, pl.ds(off, tokens)], ssem.at[d], rsem.at[d], seq, peer
        )

    v_copies = [gather_copy(v_hbm, vx, W, va_s, va_r, d) for d in range(1, n_val)]
    g_copies = [gather_copy(g_hbm, gx, 0, ga_s, ga_r, d) for d in range(1, n_val)]
    v_local = pltpu.make_async_copy(v_hbm.at[pl.ds(val * heads, heads)], vx.at[:, mine, pl.ds(W, tokens)], loc.at[0])
    g_local = pltpu.make_async_copy(g_hbm.at[pl.ds(val * heads, heads)], gx.at[:, mine, :], loc.at[1])
    key_halo = remote(
        k_ref.at[:, :, pl.ds(tokens - W, W)], kx.at[:, :, pl.ds(0, W)], kh.at[0], kh.at[1], after, val
    )
    value_halo = remote(
        vx.at[:, :, pl.ds(tokens, W)], vx.at[:, :, pl.ds(0, W)], vh.at[0], vh.at[1], after, val
    )
    key_back = remote(hk_send, hk_recv, gkh.at[0], gkh.at[1], ahead, val)
    value_back = remote(hv_send, hv_recv, gvh.at[0], gvh.at[1], ahead, val)

    @pl.when(jnp.logical_not(last))
    def _():
        key_halo.start()

    for c in v_copies:
        c.start()
    v_local.start()
    for c in g_copies:
        c.start()
    g_local.start()

    const = jnp.where(lax.broadcasted_iota(jnp.int32, (FR - LIN - 16, tokens), 0) == 0, 1.0, 0.0).astype(BF16)

    def build_features(src, dst):
        def one(h, carry):
            xs = src[h].astype(F32) * 0.5
            for d in range(9):
                dst[h, 16 * d : 16 * d + 16, :] = (xs * turn_up(xs, d) * ROOT_HALF).astype(BF16)
            dst[h, LIN : LIN + 16, :] = xs.astype(BF16)
            dst[h, LIN + 16 :, :] = const
            return carry

        lax.fori_loop(0, heads, one, 0)

    build_features(k_ref, fk)
    ones = jnp.ones((16, W), BF16)
    for h in range(heads):
        total = jnp.zeros((1, FR), F32)
        for b in range(blocks):
            row = nt(ones, fk[h, :, b * W : (b + 1) * W])[:1]
            nrow[h, b, :1] = row
            total = total + row
        nsend[h : h + 1, :] = total

    def vector_x(send, buf, ssem, rsem):
        buf[x] = send[...]
        return [remote(send, buf.at[x], ssem.at[d], rsem.at[d], x_peer(d), val) for d in range(1, NX)]

    nsend[heads:, :] = jnp.zeros((8 - heads, FR), F32)
    n_x = vector_x(nsend, nxbuf, nxs, nxr)
    for c in n_x:
        c.start()
    build_features(q_ref, fq)

    row_id = lax.broadcasted_iota(jnp.int32, (CH, CH), 0)
    col_id = lax.broadcasted_iota(jnp.int32, (CH, CH), 1)

    def scores(h, b):
        mask = row_id <= col_id
        for half in range(2):
            t0 = b * W + half * CH
            qs = (q_ref[h, :, t0 : t0 + CH].astype(F32) * 0.25).astype(BF16)
            s = tn(kx[h, :, t0 : t0 + 3 * CH], qs)
            s_old, s_mid, s_own = s[:CH], s[CH : 2 * CH], s[2 * CH :]
            w_mid = s_mid
            if b == 0:
                gone = jnp.where(first, NEG_LARGE, 0.0)
                s_old = s_old + gone
                if half == 0:
                    w_mid = s_mid + gone
            s_diag = jnp.where(mask, s_own, s_old)
            top = jnp.maximum(
                jnp.max(s_diag, axis=0, keepdims=True), jnp.max(w_mid, axis=0, keepdims=True)
            )
            e_diag = jnp.exp(s_diag - top)
            e_mid = jnp.exp(w_mid - top)
            sums = jnp.sum(e_diag, axis=0, keepdims=True) + jnp.sum(e_mid, axis=0, keepdims=True)
            scale = 1.0 / sums
            p_diag = e_diag * scale
            es[h, b, half, :CH] = jnp.where(mask, 0.0, p_diag).astype(BF16)
            es[h, b, half, CH : 2 * CH] = (e_mid * scale).astype(BF16)
            es[h, b, half, 2 * CH :] = jnp.where(mask, p_diag, 0.0).astype(BF16)
            c_own = 1.0 + s_own
            t_own = jnp.where(mask, 0.5 * (c_own * c_own) + 0.5, 0.0)
            den = jnp.sum(t_own, axis=0, keepdims=True)
            cs[h, b, half, CH:] = jnp.where(mask, c_own, 0.0).astype(BF16)
            ts[h, b, half, CH:] = t_own.astype(BF16)
            if half == 1:
                c_mid = 1.0 + s_mid
                t_mid = 0.5 * (c_mid * c_mid) + 0.5
                den = den + jnp.sum(t_mid, axis=0, keepdims=True)
                cs[h, b, half, :CH] = c_mid.astype(BF16)
                ts[h, b, half, :CH] = t_mid.astype(BF16)
            deni[h, b, :1, half * CH : (half + 1) * CH] = den

    def each_head(body):
        def one(h, carry):
            body(h)
            return carry

        lax.fori_loop(0, heads, one, 0)

    for b in range(1, blocks):
        each_head(functools.partial(lambda h, b: scores(h, b), b=b))

    def vector_z(tot, buf, ssem, rsem, d, forward):
        to = z + d if forward else z - d
        return remote(tot, buf.at[d], ssem.at[d], rsem.at[d], to * NX + x, val)

    def z_sends(d, forward):
        return (z + d < nz) if forward else (z >= d)

    def z_takes(d, forward):
        return (z >= d) if forward else (z + d < nz)

    def vector_total(copies, buf, tot):
        for c in copies:
            c.wait_recv()
        total = buf[0]
        for i in range(1, NX):
            total = total + buf[i]
        tot[...] = total

    def vector_z_start(tot, buf, ssem, rsem, forward):
        for d in range(1, nz):

            @pl.when(z_sends(d, forward))
            def _():
                vector_z(tot, buf, ssem, rsem, d, forward).start()

    def vector_end(xbuf, tot, zbuf, ssem, rsem, out, forward):
        acc = jnp.zeros((8, FR), F32)
        for i in range(NX):
            taken = (i < x) if forward else (i > x)
            acc = acc + jnp.where(taken, xbuf[i], 0.0)
        out[...] = acc
        for d in range(1, nz):

            @pl.when(z_takes(d, forward))
            def _():
                vector_z(tot, zbuf, ssem, rsem, d, forward).wait_recv()
                out[...] += zbuf[d]

    def vector_z_finish(tot, buf, ssem, rsem, forward):
        for d in range(1, nz):

            @pl.when(z_sends(d, forward))
            def _():
                vector_z(tot, buf, ssem, rsem, d, forward).wait_send()

    vector_total(n_x, nxbuf, ntot)
    vector_z_start(ntot, nzbuf, nzs, nzr, True)

    @pl.when(jnp.logical_not(first))
    def _():
        key_halo.wait_recv()

    each_head(lambda h: scores(h, 0))

    vector_end(nxbuf, ntot, nzbuf, nzs, nzr, npre, True)

    def as_column(row):
        return jnp.transpose(jnp.broadcast_to(row, (128, row.shape[1])))

    weights = pair_weights(128)
    for h in range(heads):
        row = npre[h : h + 1, :]
        for b in range(blocks):
            column = as_column(row) * weights
            ncol[h, b] = column
            den = deni[h, b, :1, :]
            for i in range(W // 128):
                lanes = slice(b * W + i * 128, b * W + (i + 1) * 128)
                inter = jnp.sum(fq[h, :, lanes].astype(F32) * column, axis=0, keepdims=True)
                part_lanes = slice(i * 128, (i + 1) * 128)
                rden[h, b, :1, part_lanes] = 1.0 / (deni[h, b, :1, part_lanes] + inter)
            row = row + nrow[h, b, :1]

    for c in v_copies:
        c.wait_recv()
    v_local.wait()

    @pl.when(jnp.logical_not(last))
    def _():
        value_halo.start()

    def matrix_send(h, total, send):
        low = total.astype(BF16)
        for i in range(NX):
            send[i, h] = low[i * QR : (i + 1) * QR]

    for h in range(heads):
        total = None
        for b in range(blocks):
            term = nt(fk[h, :, b * W : (b + 1) * W], vx[h, :, W + b * W : W + (b + 1) * W])
            s_blk[h, b] = term
            total = term if total is None else total + term
        matrix_send(h, total, s_send)

    def matrix_x(send, buf, ssem, rsem):
        return [
            remote(send.at[lax.rem(x + d, NX)], buf.at[x], ssem.at[d], rsem.at[d], x_peer(d), val)
            for d in range(1, NX)
        ]

    def matrix_total(copies, send, buf, tot):
        for c in copies:
            c.wait_recv()
        total = buf[0].astype(F32)
        for i in range(1, NX):
            total = total + buf[i].astype(F32)
        tot[...] = total.astype(BF16)

    def matrix_end(buf, tot, zbuf, ssem, rsem, acc, out, forward):
        acc[...] = jnp.zeros(acc.shape, F32)
        for d in range(1, nz):

            @pl.when(z_takes(d, forward))
            def _():
                vector_z(tot, zbuf, ssem, rsem, d, forward).wait_recv()
                acc[...] += zbuf[d].astype(F32)

        running = acc[...]
        order = range(NX) if forward else range(NX - 1, -1, -1)
        for i in order:
            out[i] = running.astype(BF16)
            running = running + buf[i].astype(F32)

    def matrix_out(out, pre, ssem, rsem):
        pre[x] = out[x]
        return [
            remote(out.at[lax.rem(x + d, NX)], pre.at[x], ssem.at[d], rsem.at[d], x_peer(d), val)
            for d in range(1, NX)
        ]

    s_x[x] = s_send[x]
    s_1 = matrix_x(s_send, s_x, sxs, sxr)
    for c in s_1:
        c.start()

    def scores_values(h):
        for b in range(blocks):
            for half in range(2):
                lo = 0 if half else CH
                own = slice(W + b * W, W + b * W + (half + 1) * CH)
                cols = slice(b * W + half * CH, b * W + (half + 1) * CH)
                num[h, :, cols] = nn(vx[h, :, own], ts[h, b, half, lo:])
                kc[h, :, cols] = nn(kx[h, :, own], cs[h, b, half, lo:])

    each_head(scores_values)

    def windows(h, b):
        for half in range(2):
            t0 = b * W + half * CH
            win[h, :, t0 : t0 + CH] = nn(vx[h, :, t0 : t0 + 3 * CH], es[h, b, half])

    for b in range(1, blocks):
        each_head(functools.partial(lambda h, b: windows(h, b), b=b))

    matrix_total(s_1, s_send, s_x, s_tot)
    vector_z_start(s_tot, s_z, szs, szr, True)

    for c in g_copies:
        c.wait_recv()
    g_local.wait()

    def scale_grads(h):
        for b in range(blocks):
            cols = slice(b * W, (b + 1) * W)
            wide = gx[h, :, cols].astype(F32)
            dn[h, :, cols] = (wide * rden[h, b, :1]).astype(BF16)

    each_head(scale_grads)
    for h in range(heads):
        total = None
        for b in range(blocks):
            term = nt(fq[h, :, b * W : (b + 1) * W], dn[h, :, b * W : (b + 1) * W])
            u_blk[h, b] = term
            total = term if total is None else total + term
        matrix_send(h, total, u_send)
    u_x[x] = u_send[x]
    u_1 = matrix_x(u_send, u_x, uxs, uxr)
    for c in u_1:
        c.start()

    @pl.when(jnp.logical_not(first))
    def _():
        value_halo.wait_recv()

    each_head(lambda h: windows(h, 0))

    def turn_values(h):
        for i in range(vx.shape[2] // CH):
            vt[h, i * CH : (i + 1) * CH] = jnp.transpose(vx[h, :, i * CH : (i + 1) * CH].astype(F32)).astype(BF16)

    each_head(turn_values)

    def deltas(h):
        for b in range(blocks):
            cols = slice(b * W, (b + 1) * W)
            dl[h, b, :1] = jnp.sum(gx[h, :, cols].astype(F32) * win[h, :, cols], axis=0, keepdims=True)

    each_head(deltas)

    dka[...] = jnp.zeros(dka.shape, F32)
    dva[...] = jnp.zeros(dva.shape, F32)

    def backward(h, b):
        for half in range(2):
            lo = 0 if half else CH
            t0 = b * W + half * CH
            cols = slice(t0, t0 + CH)
            keys = slice(t0, t0 + 3 * CH)
            own = slice(W + b * W, W + b * W + (half + 1) * CH)
            count = (half + 1) * CH
            mixing = nn(vt[h, keys], gx[h, :, cols])
            mixing_dn = nn(vt[h, own], dn[h, :, cols])
            e = es[h, b, half]
            gs = e.astype(F32) * (mixing - dl[h, b, :1, half * CH : (half + 1) * CH])
            taylor = cs[h, b, half, lo:].astype(F32) * mixing_dn
            gs = jnp.concatenate([gs[: 3 * CH - count], gs[3 * CH - count :] + taylor], axis=0).astype(BF16)
            dqa[h, :, cols] = nn(kx[h, :, keys], gs)
            dka[h, :, keys] += nt(q_ref[h, :, cols], gs)
            dva[h, :, keys] += nt(gx[h, :, cols], e)
            dva[h, :, own] += nt(dn[h, :, cols], ts[h, b, half, lo:])

    each_head(lambda h: backward(h, 0))
    hk_send[...] = (0.25 * dka[:, :, :W]).astype(BF16)
    hv_send[...] = dva[:, :, :W].astype(BF16)

    @pl.when(jnp.logical_not(first))
    def _():
        key_back.start()
        value_back.start()

    matrix_end(s_x, s_tot, s_z, szs, szr, s_acc, s_out, True)
    s_3 = matrix_out(s_out, s_pre, sos, sor)
    for c in s_3:
        c.start()
    matrix_total(u_1, u_send, u_x, u_tot)
    vector_z_start(u_tot, u_z, uzs, uzr, False)

    for b in range(1, blocks):
        each_head(functools.partial(lambda h, b: backward(h, b), b=b))

    for c in s_3:
        c.wait_recv()

    def whole(pre, h):
        return jnp.concatenate([pre[i, h].astype(F32) for i in range(NX)], axis=0)

    def fold(grad, rows):
        xs = rows.astype(F32) * 0.5
        acc = 2.0 * (grad[:16] * xs + grad[128:144] * turn_up(xs, 8))
        for d in range(1, 8):
            one = grad[16 * d : 16 * d + 16]
            acc = acc + one * turn_up(xs, d) + turn_down(one * xs, d)
        return 0.5 * grad[LIN : LIN + 16] + (0.5 * ROOT_HALF) * acc

    def forward_end(h):
        state = whole(s_pre, h)
        for b in range(blocks):
            if b:
                state = state + s_blk[h, b - 1]
            low = (state * weights).astype(BF16)
            cols = slice(b * W, (b + 1) * W)
            scale = rden[h, b, :1]
            lin = (num[h, :, cols] + tn(low, fq[h, :, cols])) * scale
            mix[h, :, cols] = (lin + win[h, :, cols]).astype(BF16)
            d_row = -jnp.sum(gx[h, :, cols].astype(F32) * lin, axis=0, keepdims=True) * scale
            dd[h, b, :1] = d_row
            drow[h, b, :1] = jnp.sum(nt(split_rows(d_row), fq[h, :, cols]), axis=0, keepdims=True)
            grad = nn(low, dn[h, :, cols])
            column = ncol[h, b]
            grad = grad + jnp.concatenate([column] * (W // 128), axis=1) * d_row
            local = dqa[h, :, cols] + d_row * kc[h, :, cols]
            dq_out[h, :, cols] = 0.25 * local + fold(grad, q_ref[h, :, cols])
            qd = (q_ref[h, :, cols].astype(F32) * d_row).astype(BF16)
            for half in range(2):
                lo = 0 if half else CH
                own = slice(W + b * W, W + b * W + (half + 1) * CH)
                dka[h, :, own] += nt(qd[:, half * CH : (half + 1) * CH], cs[h, b, half, lo:])

    each_head(forward_end)

    def scatter(src, dst, ssem, rsem, d):
        peer = val_peer(d)
        return remote(
            src.at[:, pl.ds(pl.multiple_of(peer * part, part), part), :],
            dst.at[pl.ds(val * heads, heads)],
            ssem.at[d],
            rsem.at[d],
            seq,
            peer,
        )

    m_copies = [scatter(mix, mixed_out, mo_s, mo_r, d) for d in range(1, n_val)]
    m_local = pltpu.make_async_copy(mix.at[:, mine, :], mixed_out.at[pl.ds(val * heads, heads)], loc.at[2])
    for c in m_copies:
        c.start()
    m_local.start()

    for h in range(heads):
        total = drow[h, 0, :1]
        for b in range(1, blocks):
            total = total + drow[h, b, :1]
        dsend[h : h + 1, :] = total
    dsend[heads:, :] = jnp.zeros((8 - heads, FR), F32)
    d_x = vector_x(dsend, dxbuf, dxs, dxr)
    for c in d_x:
        c.start()

    matrix_end(u_x, u_tot, u_z, uzs, uzr, u_acc, u_out, False)
    u_3 = matrix_out(u_out, u_pre, uos, uor)
    for c in u_3:
        c.start()

    vector_total(d_x, dxbuf, dtot)
    vector_z_start(dtot, dzbuf, dzs, dzr, False)

    @pl.when(jnp.logical_not(last))
    def _():
        key_back.wait_recv()
        value_back.wait_recv()
        dka[:, :, tokens:] += 4.0 * hk_recv[...].astype(F32)
        dva[:, :, tokens:] += hv_recv[...].astype(F32)

    for c in u_3:
        c.wait_recv()

    def suffix_of(h, b):
        state = whole(u_pre, h)
        for i in range(b + 1, blocks):
            state = state + u_blk[h, i]
        return (state * weights).astype(BF16)

    def value_end(h):
        for b in range(blocks):
            cols = slice(b * W, (b + 1) * W)
            inter = tn(suffix_of(h, b), fk[h, :, cols])
            dvb[h, :, cols] = (dva[h, :, W + b * W : W + (b + 1) * W] + inter).astype(BF16)

    each_head(value_end)
    d_copies = [scatter(dvb, dv_out, do_s, do_r, d) for d in range(1, n_val)]
    d_local = pltpu.make_async_copy(dvb.at[:, mine, :], dv_out.at[pl.ds(val * heads, heads)], loc.at[3])
    for c in d_copies:
        c.start()
    d_local.start()

    vector_end(dxbuf, dtot, dzbuf, dzs, dzr, dsuf, False)

    for h in range(heads):
        row = dsuf[h : h + 1, :]
        for b in range(blocks - 1, -1, -1):
            cols = slice(b * W, (b + 1) * W)
            column = as_column(row) * weights
            grad = nn(suffix_of(h, b), vx[h, :, W + b * W : W + (b + 1) * W])
            grad = grad + jnp.concatenate([column] * (W // 128), axis=1)
            dk_out[h, :, cols] = 0.25 * dka[h, :, W + b * W : W + (b + 1) * W] + fold(grad, k_ref[h, :, cols])
            row = row + drow[h, b, :1]

    for c in v_copies + g_copies + n_x + d_x + s_1 + u_1 + s_3 + u_3:
        c.wait_send()
    for c in m_copies + d_copies:
        c.wait()
    m_local.wait()
    d_local.wait()

    @pl.when(jnp.logical_not(last))
    def _():
        key_halo.wait_send()
        value_halo.wait_send()

    @pl.when(jnp.logical_not(first))
    def _():
        key_back.wait_send()
        value_back.wait_send()

    vector_z_finish(ntot, nzbuf, nzs, nzr, True)
    vector_z_finish(s_tot, s_z, szs, szr, True)
    vector_z_finish(u_tot, u_z, uzs, uzr, False)
    vector_z_finish(dtot, dzbuf, dzs, dzr, False)


def local(queries, keys, values, out_grad):
    heads, width, tokens = queries.shape
    all_heads, part, _ = values.shape
    n_seq, n_val = lax.axis_size("seq"), lax.axis_size("val")
    nz = n_seq // NX
    blocks = tokens // W
    ev = part * n_val
    vm = pltpu.VMEM
    dma = pltpu.SemaphoreType.DMA
    row = (heads, blocks, 8, W)

    def matrix_scratch():
        return [
            vm((heads, blocks, FR, ev), F32),
            vm((NX, heads, QR, ev), BF16),
            vm((NX, heads, QR, ev), BF16),
            vm((heads, QR, ev), BF16),
            vm((nz, heads, QR, ev), BF16),
            vm((heads, QR, ev), F32),
            vm((NX, heads, QR, ev), BF16),
            vm((NX, heads, QR, ev), BF16),
        ]

    def vector_scratch():
        return [
            vm((8, FR), F32),
            vm((NX, 8, FR), F32),
            vm((8, FR), F32),
            vm((nz, 8, FR), F32),
            vm((8, FR), F32),
        ]

    scratch = [
        vm((heads, width, W + tokens), BF16),
        vm((heads, ev, W + tokens), BF16),
        vm((heads, W + tokens, ev), BF16),
        vm((heads, ev, tokens), BF16),
        vm((heads, FR, tokens), BF16),
        vm((heads, FR, tokens), BF16),
        vm((heads, blocks, 2, 3 * CH, CH), BF16),
        vm((heads, blocks, 2, 2 * CH, CH), BF16),
        vm((heads, blocks, 2, 2 * CH, CH), BF16),
        vm((heads, ev, tokens), F32),
        vm((heads, ev, tokens), F32),
        vm((heads, width, tokens), F32),
        vm(row, F32),
        vm(row, F32),
        vm(row, F32),
        vm(row, F32),
        vm((heads, ev, tokens), BF16),
        vm((heads, width, tokens), F32),
        vm((heads, width, W + tokens), F32),
        vm((heads, ev, W + tokens), F32),
        vm((heads, ev, tokens), BF16),
        vm((heads, ev, tokens), BF16),
        vm((heads, blocks, 8, FR), F32),
        *vector_scratch(),
        vm((heads, blocks, FR, 128), F32),
        vm((heads, blocks, 8, FR), F32),
        *vector_scratch(),
        *matrix_scratch(),
        *matrix_scratch(),
        vm((heads, width, W), BF16),
        vm((heads, ev, W), BF16),
        vm((heads, width, W), BF16),
        vm((heads, ev, W), BF16),
        *[dma((n_val,)) for _ in range(8)],
        dma((4,)),
        *[dma((2,)) for _ in range(4)],
        *[dma((NX,)), dma((NX,)), dma((nz,)), dma((nz,))] * 2,
        *[dma((NX,)), dma((NX,)), dma((nz,)), dma((nz,)), dma((NX,)), dma((NX,))] * 2,
    ]
    vmem = pl.BlockSpec(memory_space=pltpu.VMEM)
    hbm = pl.BlockSpec(memory_space=pl.ANY)
    return pl.pallas_call(
        functools.partial(kernel, n_seq, n_val),
        out_shape=(
            jax.ShapeDtypeStruct(values.shape, BF16),
            jax.ShapeDtypeStruct(queries.shape, F32),
            jax.ShapeDtypeStruct(keys.shape, F32),
            jax.ShapeDtypeStruct(values.shape, BF16),
        ),
        in_specs=[vmem, vmem, hbm, hbm],
        out_specs=(hbm, vmem, vmem, hbm),
        scratch_shapes=scratch,
        compiler_params=pltpu.CompilerParams(
            collective_id=0, has_side_effects=True, vmem_limit_bytes=56 << 20
        ),
        name="based_layer",
    )(queries, keys, values, out_grad)


def solution(mesh):
    in_specs = (
        P("val", None, "seq"),
        P("val", None, "seq"),
        P(None, "val", "seq"),
        P(None, "val", "seq"),
    )
    out_specs = (
        P(None, "val", "seq"),
        P("val", None, "seq"),
        P("val", None, "seq"),
        P(None, "val", "seq"),
    )
    return jax.shard_map(local, mesh=mesh, in_specs=in_specs, out_specs=out_specs, check_vma=False)
```

```python
import functools

import jax
import jax.numpy as jnp
from jax import lax
from jax.experimental import pallas as pl
from jax.experimental.pallas import tpu as pltpu
from jax.sharding import PartitionSpec as P

W = 512
CH = 256
NX = 4
FR = 192
QR = FR // NX
LIN = 144
ROOT_HALF = 0.7071067811865476
NEG_LARGE = -1e30
MESH = pl.DeviceIdType.MESH
F32 = jnp.float32
BF16 = jnp.bfloat16


def dot(a, b, ca, cb):
    return lax.dot_general(a, b, (((ca,), (cb,)), ((), ())), preferred_element_type=F32)


def nn(a, b):
    return dot(a, b, 1, 0)


def nt(a, b):
    return dot(a, b, 1, 1)


def tn(a, b):
    return dot(a, b, 0, 0)


def turn_up(x, d):
    return jnp.concatenate([x[d:], x[:d]], axis=0) if d else x


def turn_down(x, d):
    return turn_up(x, 16 - d)


def split_rows(row):
    high = row.astype(BF16).astype(F32)
    low = row - high
    index = lax.broadcasted_iota(jnp.int32, (16, row.shape[1]), 0)
    return jnp.where(index == 0, high, jnp.where(index == 1, low, 0.0)).astype(BF16)


def when(condition, action):
    if condition is None:
        action()
    else:
        pl.when(condition)(action)


class Copy:
    def __init__(self, started, make, sends=None, takes=None):
        self.started, self.make, self.sends, self.takes = started, make, sends, takes
        self.waits = {"send", "recv"}

    def start(self):
        when(self.sends, lambda: self.make().start())
        self.started.append(self)

    def wait_recv(self):
        self.waits.discard("recv")
        when(self.takes, lambda: self.make().wait_recv())

    def finish(self):
        if "recv" in self.waits:
            self.wait_recv()
        when(self.sends, lambda: self.make().wait_send())


class Local:
    def __init__(self, started, copy):
        self.started, self.copy, self.waiting = started, copy, True

    def start(self):
        self.copy.start()
        self.started.append(self)

    def wait_recv(self):
        self.waiting = False
        self.copy.wait()

    def finish(self):
        if self.waiting:
            self.wait_recv()


def start(copies):
    for c in copies:
        c.start()


def take(copies):
    for c in copies:
        c.wait_recv()


def pair_weights(columns):
    row = lax.broadcasted_iota(jnp.int32, (FR, columns), 0)
    return jnp.where(jnp.logical_and(row >= 16, row < 128), 2.0, 1.0)


def kernel(
    n_seq,
    n_val,
    q_hbm,
    k_hbm,
    v_hbm,
    g_hbm,
    mixed_out,
    dq_out,
    dk_out,
    dv_out,
    q_ref,
    kx,
    vx,
    vt,
    gx,
    fq,
    fk,
    es,
    cs,
    ts,
    num,
    win,
    kc,
    deni,
    rden,
    dd,
    dl,
    dn,
    dqa,
    dka,
    dva,
    mix,
    dvb,
    nrow,
    nsend,
    nxbuf,
    ntot,
    nzbuf,
    npre,
    ncol,
    drow,
    dsend,
    dxbuf,
    dtot,
    dzbuf,
    dsuf,
    s_blk,
    s_send,
    s_x,
    s_tot,
    s_z,
    s_acc,
    s_out,
    s_pre,
    u_blk,
    u_send,
    u_x,
    u_tot,
    u_z,
    u_acc,
    u_out,
    u_pre,
    hk_send,
    hv_send,
    hk_recv,
    hv_recv,
    va_s,
    va_r,
    ga_s,
    ga_r,
    mo_s,
    mo_r,
    do_s,
    do_r,
    loc,
    vloc,
    gloc,
    mloc,
    dloc,
    kh,
    vh,
    gkh,
    gvh,
    nxs,
    nxr,
    nzs,
    nzr,
    dxs,
    dxr,
    dzs,
    dzr,
    sxs,
    sxr,
    szs,
    szr,
    sos,
    sor,
    uxs,
    uxr,
    uzs,
    uzr,
    uos,
    uor,
):
    heads = q_ref.shape[0]
    tokens = q_ref.shape[2]
    blocks = tokens // W
    part = v_hbm.shape[1]
    nz = n_seq // NX
    seq = lax.axis_index("seq")
    val = lax.axis_index("val")
    z = seq // NX
    x = lax.rem(seq, NX)
    first = seq == 0
    last = seq == n_seq - 1
    after = lax.rem(seq + 1, n_seq)
    ahead = lax.rem(seq + n_seq - 1, n_seq)

    started = []

    def remote(src, dst, ssem, rsem, s, v, sends=None, takes=None):
        def make():
            return pltpu.make_async_remote_copy(
                src_ref=src, dst_ref=dst, send_sem=ssem, recv_sem=rsem, device_id=(s, v), device_id_type=MESH
            )

        return Copy(started, make, sends, takes)

    def drain():
        for c in started:
            c.finish()

    def val_peer(d):
        return lax.rem(val + d, n_val)

    def x_peer(d):
        return z * NX + lax.rem(x + d, NX)

    k_load = pltpu.make_async_copy(k_hbm, kx.at[:, :, pl.ds(W, tokens)], loc.at[0])
    q_load = pltpu.make_async_copy(q_hbm, q_ref, loc.at[1])
    k_load.start()
    q_load.start()
    barrier = pltpu.get_barrier_semaphore()

    def greet(s, v):
        pl.semaphore_signal(barrier, inc=1, device_id=(s, v), device_id_type=MESH)

    for d in range(1, n_val):
        greet(seq, val_peer(d))
    for d in range(1, NX):
        greet(x_peer(d), val)
    for d in range(1, nz):
        greet(lax.rem(z + d, nz) * NX + x, val)
    greet(after, val)
    greet(ahead, val)

    @pl.when(first)
    def _():
        kx[:, :, :W] = jnp.zeros((heads, 16, W), BF16)
        vx[:, :, :W] = jnp.zeros((heads, 128, W), BF16)

    k_load.wait()
    q_load.wait()
    pl.semaphore_wait(barrier, (n_val - 1) + (NX - 1) + (nz - 1) + 2)

    mine = pl.ds(pl.multiple_of(val * part, part), part)
    my_heads = pl.ds(val * heads, heads)

    def gather_copies(src, dst, off, ssem, rsem, lsem, b):
        copies = []
        span = pl.ds(b * W, W)
        for d in range(1, n_val):
            peer = val_peer(d)
            copies.append(
                remote(
                    src.at[pl.ds(peer * heads, heads), :, span],
                    dst.at[:, mine, pl.ds(off + b * W, W)],
                    ssem.at[b, d],
                    rsem.at[b, d],
                    seq,
                    peer,
                )
            )
        copies.append(
            Local(started, pltpu.make_async_copy(src.at[my_heads, :, span], dst.at[:, mine, pl.ds(off + b * W, W)], lsem.at[b]))
        )
        return copies

    v_copies = [gather_copies(v_hbm, vx, W, va_s, va_r, vloc, b) for b in range(blocks)]
    g_copies = [gather_copies(g_hbm, gx, 0, ga_s, ga_r, gloc, b) for b in range(blocks)]
    inner, outer = jnp.logical_not(first), jnp.logical_not(last)
    key_halo = remote(
        kx.at[:, :, pl.ds(tokens, W)], kx.at[:, :, pl.ds(0, W)], kh.at[0], kh.at[1], after, val, outer, inner
    )
    value_halo = remote(
        vx.at[:, :, pl.ds(tokens, W)], vx.at[:, :, pl.ds(0, W)], vh.at[0], vh.at[1], after, val, outer, inner
    )
    key_back = remote(hk_send, hk_recv, gkh.at[0], gkh.at[1], ahead, val, inner, outer)
    value_back = remote(hv_send, hv_recv, gvh.at[0], gvh.at[1], ahead, val, inner, outer)
    start(v_copies[blocks - 1])
    key_halo.start()
    for b in range(blocks - 1):
        start(v_copies[b])

    const = jnp.where(lax.broadcasted_iota(jnp.int32, (FR - LIN - 16, tokens), 0) == 0, 1.0, 0.0).astype(BF16)
    row_id = lax.broadcasted_iota(jnp.int32, (CH, CH), 0)
    col_id = lax.broadcasted_iota(jnp.int32, (CH, CH), 1)
    weights = pair_weights(128)
    ones = jnp.ones((16, W), BF16)

    def build_features(src, off, dst):
        def one(h, carry):
            xs = src[h, :, off : off + tokens].astype(F32) * 0.5
            for d in range(9):
                dst[h, 16 * d : 16 * d + 16, :] = (xs * turn_up(xs, d) * ROOT_HALF).astype(BF16)
            dst[h, LIN : LIN + 16, :] = xs.astype(BF16)
            dst[h, LIN + 16 :, :] = const
            return carry

        lax.fori_loop(0, heads, one, 0)

    def vector_x(send, buf, ssem, rsem):
        buf[x] = send[...]
        return [remote(send, buf.at[x], ssem.at[d], rsem.at[d], x_peer(d), val) for d in range(1, NX)]

    def scores(h, b):
        mask = row_id <= col_id
        for half in range(2):
            t0 = b * W + half * CH
            qs = (q_ref[h, :, t0 : t0 + CH].astype(F32) * 0.25).astype(BF16)
            s = tn(kx[h, :, t0 : t0 + 3 * CH], qs)
            s_old, s_mid, s_own = s[:CH], s[CH : 2 * CH], s[2 * CH :]
            w_mid = s_mid
            if b == 0:
                gone = jnp.where(first, NEG_LARGE, 0.0)
                s_old = s_old + gone
                if half == 0:
                    w_mid = s_mid + gone
            s_diag = jnp.where(mask, s_own, s_old)
            top = jnp.maximum(
                jnp.max(s_diag, axis=0, keepdims=True), jnp.max(w_mid, axis=0, keepdims=True)
            )
            e_diag = jnp.exp(s_diag - top)
            e_mid = jnp.exp(w_mid - top)
            sums = jnp.sum(e_diag, axis=0, keepdims=True) + jnp.sum(e_mid, axis=0, keepdims=True)
            scale = 1.0 / sums
            p_diag = e_diag * scale
            es[h, b, half, :CH] = jnp.where(mask, 0.0, p_diag).astype(BF16)
            es[h, b, half, CH : 2 * CH] = (e_mid * scale).astype(BF16)
            es[h, b, half, 2 * CH :] = jnp.where(mask, p_diag, 0.0).astype(BF16)
            c_own = 1.0 + s_own
            t_own = jnp.where(mask, 0.5 * (c_own * c_own) + 0.5, 0.0)
            den = jnp.sum(t_own, axis=0, keepdims=True)
            cs[h, b, half, CH:] = jnp.where(mask, c_own, 0.0).astype(BF16)
            ts[h, b, half, CH:] = t_own.astype(BF16)
            if half == 1:
                c_mid = 1.0 + s_mid
                t_mid = 0.5 * (c_mid * c_mid) + 0.5
                den = den + jnp.sum(t_mid, axis=0, keepdims=True)
                cs[h, b, half, :CH] = c_mid.astype(BF16)
                ts[h, b, half, :CH] = t_mid.astype(BF16)
            deni[h, b, :1, half * CH : (half + 1) * CH] = den

    def each_head(body):
        def one(h, carry):
            body(h)
            return carry

        lax.fori_loop(0, heads, one, 0)

    def along_z(tot, buf, ssem, rsem, forward):
        copies = []
        for d in range(1, nz):
            to = z + d if forward else z - d
            up, down = z + d < nz, z >= d
            sends, takes = (up, down) if forward else (down, up)
            copies.append(remote(tot, buf.at[d], ssem.at[d], rsem.at[d], to * NX + x, val, sends, takes))
            copies[-1].start()
        return copies

    def vector_total(copies, buf, tot):
        for c in copies:
            c.wait_recv()
        total = buf[0]
        for i in range(1, NX):
            total = total + buf[i]
        tot[...] = total

    def vector_end(xbuf, copies, zbuf, out, forward):
        acc = jnp.zeros((8, FR), F32)
        for i in range(NX):
            taken = (i < x) if forward else (i > x)
            acc = acc + jnp.where(taken, xbuf[i], 0.0)
        out[...] = acc
        add_arrivals(copies, zbuf, out)

    def add_arrivals(copies, zbuf, out):
        for i, c in enumerate(copies):
            c.wait_recv()

            def add():
                out[...] += zbuf[i + 1].astype(F32)

            when(c.takes, add)

    def as_column(row):
        return jnp.transpose(jnp.broadcast_to(row, (128, row.shape[1])))

    def matrix_send(h, total, send):
        low = total.astype(BF16)
        for i in range(NX):
            send[i, h] = low[i * QR : (i + 1) * QR]

    def matrix_x(send, buf, ssem, rsem):
        return [
            remote(send.at[lax.rem(x + d, NX)], buf.at[x], ssem.at[d], rsem.at[d], x_peer(d), val)
            for d in range(1, NX)
        ]

    def matrix_total(copies, send, buf, tot):
        for c in copies:
            c.wait_recv()
        total = buf[0].astype(F32)
        for i in range(1, NX):
            total = total + buf[i].astype(F32)
        tot[...] = total.astype(BF16)

    def matrix_end(buf, copies, zbuf, acc, out, forward):
        acc[...] = jnp.zeros(acc.shape, F32)
        add_arrivals(copies, zbuf, acc)
        running = acc[...]
        order = range(NX) if forward else range(NX - 1, -1, -1)
        for i in order:
            out[i] = running.astype(BF16)
            running = running + buf[i].astype(F32)

    def matrix_out(out, pre, ssem, rsem):
        pre[x] = out[x]
        return [
            remote(out.at[lax.rem(x + d, NX)], pre.at[x], ssem.at[d], rsem.at[d], x_peer(d), val)
            for d in range(1, NX)
        ]

    def scores_values(h):
        for b in range(blocks):
            for half in range(2):
                lo = 0 if half else CH
                own = slice(W + b * W, W + b * W + (half + 1) * CH)
                cols = slice(b * W + half * CH, b * W + (half + 1) * CH)
                num[h, :, cols] = nn(vx[h, :, own], ts[h, b, half, lo:])
                kc[h, :, cols] = nn(kx[h, :, own], cs[h, b, half, lo:])

    def windows(h, b):
        for half in range(2):
            t0 = b * W + half * CH
            win[h, :, t0 : t0 + CH] = nn(vx[h, :, t0 : t0 + 3 * CH], es[h, b, half])

    def scale_grads(h):
        for b in range(blocks):
            cols = slice(b * W, (b + 1) * W)
            wide = gx[h, :, cols].astype(F32)
            dn[h, :, cols] = (wide * rden[h, b, :1]).astype(BF16)

    def halo_values(h):
        for i in range(2):
            total = nt(gx[h, :, :CH], es[h, 0, 0, i * CH : (i + 1) * CH])
            if i == 1:
                total = total + nt(gx[h, :, CH:W], es[h, 0, 1, :CH])
            hv_send[h, :, i * CH : (i + 1) * CH] = total.astype(BF16)

    def turn_values(h, lo):
        for i in range(lo // CH, (vx.shape[2] if lo else W) // CH):
            vt[h, i * CH : (i + 1) * CH] = jnp.transpose(vx[h, :, i * CH : (i + 1) * CH].astype(F32)).astype(BF16)

    def deltas(h):
        for b in range(blocks):
            cols = slice(b * W, (b + 1) * W)
            dl[h, b, :1] = jnp.sum(gx[h, :, cols].astype(F32) * win[h, :, cols], axis=0, keepdims=True)

    def whole(pre, h):
        return jnp.concatenate([pre[i, h].astype(F32) for i in range(NX)], axis=0)

    def fold(grad, rows):
        xs = rows.astype(F32) * 0.5
        acc = 2.0 * (grad[:16] * xs + grad[128:144] * turn_up(xs, 8))
        for d in range(1, 8):
            one = grad[16 * d : 16 * d + 16]
            acc = acc + one * turn_up(xs, d) + turn_down(one * xs, d)
        return 0.5 * grad[LIN : LIN + 16] + (0.5 * ROOT_HALF) * acc

    def forward_state(h, b):
        state = whole(s_pre, h)
        for i in range(b):
            state = state + s_blk[h, i]
        return (state * weights).astype(BF16)

    def scatter(src, dst, ssem, rsem, lsem, b):
        copies = []
        span = pl.ds(b * W, W)
        for d in range(1, n_val):
            peer = val_peer(d)
            rows = pl.ds(pl.multiple_of(peer * part, part), part)
            copies.append(
                remote(src.at[:, rows, span], dst.at[my_heads, :, span], ssem.at[b, d], rsem.at[b, d], seq, peer)
            )
        copies.append(Local(started, pltpu.make_async_copy(src.at[:, mine, span], dst.at[my_heads, :, span], lsem.at[b])))
        return copies

    def query_end(h):
        for b in range(blocks):
            cols = slice(b * W, (b + 1) * W)
            d_row = dd[h, b, :1]
            grad = nn(forward_state(h, b), dn[h, :, cols])
            grad = grad + jnp.concatenate([ncol[h, b]] * (W // 128), axis=1) * d_row
            local = dqa[h, :, cols] + d_row * kc[h, :, cols]
            dq_out[h, :, cols] = 0.25 * local + fold(grad, q_ref[h, :, cols])
            qd = (q_ref[h, :, cols].astype(F32) * d_row).astype(BF16)
            for half in range(2):
                lo = 0 if half else CH
                own = slice(W + b * W, W + b * W + (half + 1) * CH)
                dka[h, :, own] += nt(qd[:, half * CH : (half + 1) * CH], cs[h, b, half, lo:])

    def suffix_of(h, b):
        state = whole(u_pre, h)
        for i in range(b + 1, blocks):
            state = state + u_blk[h, i]
        return (state * weights).astype(BF16)

    def value_end(h, b):
        cols = slice(b * W, (b + 1) * W)
        inter = tn(suffix_of(h, b), fk[h, :, cols])
        dvb[h, :, cols] = (dva[h, :, cols] + inter).astype(BF16)

    def norm_rows():
        for h in range(heads):
            total = jnp.zeros((1, FR), F32)
            for b in range(blocks):
                row = nt(ones, fk[h, :, b * W : (b + 1) * W])[:1]
                nrow[h, b, :1] = row
                total = total + row
            nsend[h : h + 1, :] = total
        nsend[heads:, :] = jnp.zeros((8 - heads, FR), F32)

    def denominators():
        for h in range(heads):
            row = npre[h : h + 1, :]
            for b in range(blocks):
                column = as_column(row) * weights
                ncol[h, b] = column
                for i in range(W // 128):
                    lanes = slice(b * W + i * 128, b * W + (i + 1) * 128)
                    inter = jnp.sum(fq[h, :, lanes].astype(F32) * column, axis=0, keepdims=True)
                    here = slice(i * 128, (i + 1) * 128)
                    rden[h, b, :1, here] = 1.0 / (deni[h, b, :1, here] + inter)
                row = row + nrow[h, b, :1]

    def state_terms(feats, rows, off, blk, send):
        for h in range(heads):
            total = None
            for b in range(blocks):
                term = nt(feats[h, :, b * W : (b + 1) * W], rows[h, :, off + b * W : off + (b + 1) * W])
                blk[h, b] = term
                total = term if total is None else total + term
            matrix_send(h, total, send)

    def value_local(h, b):
        base = b * W
        total = nt(gx[h, :, base : base + CH], es[h, b, 0, 2 * CH :])
        total = total + nt(gx[h, :, base + CH : base + W], es[h, b, 1, CH : 2 * CH])
        total = total + nt(dn[h, :, base : base + CH], ts[h, b, 0, CH:])
        total = total + nt(dn[h, :, base + CH : base + W], ts[h, b, 1, :CH])
        last_half = nt(gx[h, :, base + CH : base + W], es[h, b, 1, 2 * CH :])
        last_half = last_half + nt(dn[h, :, base + CH : base + W], ts[h, b, 1, CH:])
        if b + 1 < blocks:
            after_base = base + W
            total = total + nt(gx[h, :, after_base : after_base + CH], es[h, b + 1, 0, :CH])
            last_half = last_half + nt(gx[h, :, after_base : after_base + CH], es[h, b + 1, 0, CH : 2 * CH])
            last_half = last_half + nt(gx[h, :, after_base + CH : after_base + W], es[h, b + 1, 1, :CH])
        dva[h, :, base : base + CH] = total
        dva[h, :, base + CH : base + W] = last_half

    def score_grads(h, b):
        for half in range(2):
            lo = 0 if half else CH
            t0 = b * W + half * CH
            cols = slice(t0, t0 + CH)
            keys = slice(t0, t0 + 3 * CH)
            own = slice(W + b * W, W + b * W + (half + 1) * CH)
            count = (half + 1) * CH
            mixing = nn(vt[h, keys], gx[h, :, cols])
            mixing_dn = nn(vt[h, own], dn[h, :, cols])
            gs = es[h, b, half].astype(F32) * (mixing - dl[h, b, :1, half * CH : (half + 1) * CH])
            taylor = cs[h, b, half, lo:].astype(F32) * mixing_dn
            gs = jnp.concatenate([gs[: 3 * CH - count], gs[3 * CH - count :] + taylor], axis=0).astype(BF16)
            dqa[h, :, cols] = nn(kx[h, :, keys], gs)
            dka[h, :, keys] += nt(q_ref[h, :, cols], gs)

    def linear_out(h):
        for b in range(blocks):
            cols = slice(b * W, (b + 1) * W)
            lin = (num[h, :, cols] + tn(forward_state(h, b), fq[h, :, cols])) * rden[h, b, :1]
            num[h, :, cols] = lin
            mix[h, :, cols] = (lin + win[h, :, cols]).astype(BF16)

    def den_grads(h):
        for b in range(blocks):
            cols = slice(b * W, (b + 1) * W)
            d_row = -jnp.sum(gx[h, :, cols].astype(F32) * num[h, :, cols], axis=0, keepdims=True) * rden[h, b, :1]
            dd[h, b, :1] = d_row
            drow[h, b, :1] = jnp.sum(nt(split_rows(d_row), fq[h, :, cols]), axis=0, keepdims=True)

    def den_rows():
        for h in range(heads):
            total = drow[h, 0, :1]
            for b in range(1, blocks):
                total = total + drow[h, b, :1]
            dsend[h : h + 1, :] = total
        dsend[heads:, :] = jnp.zeros((8 - heads, FR), F32)

    def key_end(h):
        row = dsuf[h : h + 1, :]
        for b in range(blocks - 1, -1, -1):
            cols = slice(b * W, (b + 1) * W)
            own = slice(W + b * W, W + (b + 1) * W)
            column = as_column(row) * weights
            grad = nn(suffix_of(h, b), vx[h, :, own])
            grad = grad + jnp.concatenate([column] * (W // 128), axis=1)
            dk_out[h, :, cols] = 0.25 * dka[h, :, own] + fold(grad, kx[h, :, own])
            row = row + drow[h, b, :1]

    build_features(kx, W, fk)
    norm_rows()
    n_1 = vector_x(nsend, nxbuf, nxs, nxr)
    start(n_1)
    build_features(q_ref, 0, fq)
    for b in range(1, blocks):
        each_head(functools.partial(lambda h, b: scores(h, b), b=b))
    vector_total(n_1, nxbuf, ntot)
    n_2 = along_z(ntot, nzbuf, nzs, nzr, True)
    key_halo.wait_recv()
    each_head(lambda h: scores(h, 0))
    take(v_copies[blocks - 1])
    value_halo.start()
    start(g_copies[0])
    vector_end(nxbuf, n_2, nzbuf, npre, True)
    denominators()
    for b in range(blocks - 1):
        take(v_copies[b])
    for b in range(1, blocks):
        start(g_copies[b])

    state_terms(fk, vx, W, s_blk, s_send)
    s_x[x] = s_send[x]
    s_1 = matrix_x(s_send, s_x, sxs, sxr)
    start(s_1)
    each_head(scores_values)
    for b in range(1, blocks):
        each_head(functools.partial(lambda h, b: windows(h, b), b=b))
    each_head(functools.partial(turn_values, lo=W))
    matrix_total(s_1, s_send, s_x, s_tot)
    s_2 = along_z(s_tot, s_z, szs, szr, True)
    value_halo.wait_recv()
    each_head(lambda h: windows(h, 0))

    take(g_copies[0])
    each_head(halo_values)
    value_back.start()
    for b in range(1, blocks):
        take(g_copies[b])
    each_head(scale_grads)
    state_terms(fq, dn, 0, u_blk, u_send)
    u_x[x] = u_send[x]
    u_1 = matrix_x(u_send, u_x, uxs, uxr)
    start(u_1)
    matrix_end(s_x, s_2, s_z, s_acc, s_out, True)
    s_3 = matrix_out(s_out, s_pre, sos, sor)
    start(s_3)
    for b in range(blocks):
        each_head(functools.partial(lambda h, b: value_local(h, b), b=b))
    matrix_total(u_1, u_send, u_x, u_tot)
    u_2 = along_z(u_tot, u_z, uzs, uzr, False)
    take(s_3)
    each_head(linear_out)
    for b in range(blocks):
        start(scatter(mix, mixed_out, mo_s, mo_r, mloc, b))
    each_head(den_grads)
    den_rows()
    d_1 = vector_x(dsend, dxbuf, dxs, dxr)
    start(d_1)
    each_head(functools.partial(turn_values, lo=0))
    each_head(deltas)
    dka[...] = jnp.zeros(dka.shape, F32)
    matrix_end(u_x, u_2, u_z, u_acc, u_out, False)
    u_3 = matrix_out(u_out, u_pre, uos, uor)
    start(u_3)
    each_head(lambda h: score_grads(h, 0))
    hk_send[...] = (0.25 * dka[:, :, :W]).astype(BF16)
    key_back.start()
    vector_total(d_1, dxbuf, dtot)
    d_2 = along_z(dtot, dzbuf, dzs, dzr, False)
    value_back.wait_recv()

    @pl.when(outer)
    def _():
        dva[:, :, tokens - W :] += hv_recv[...].astype(F32)

    take(u_3)
    for b in range(blocks):
        each_head(functools.partial(lambda h, b: value_end(h, b), b=b))
        start(scatter(dvb, dv_out, do_s, do_r, dloc, b))

    for b in range(1, blocks):
        each_head(functools.partial(lambda h, b: score_grads(h, b), b=b))
    each_head(query_end)
    key_back.wait_recv()

    @pl.when(outer)
    def _():
        dka[:, :, tokens:] += 4.0 * hk_recv[...].astype(F32)

    vector_end(dxbuf, d_2, dzbuf, dsuf, False)
    for h in range(heads):
        key_end(h)
    drain()


def hand_on(*refs):
    count = len(refs) // 3
    take_in, give_out = refs[-1].at[0], refs[-1].at[1]
    loads, stores = [], []
    for i in range(count):
        source, target, held = refs[i], refs[count + i], refs[2 * count + i]
        loads.append(pltpu.make_async_copy(source, held, take_in.at[i]))
        stores.append(pltpu.make_async_copy(held, target, give_out.at[i]))
    for c in loads:
        c.start()
    for load, store in zip(loads, stores):
        load.wait()
        store.start()
    for c in stores:
        c.wait()


def local(queries, keys, values, out_grad):
    heads, width, tokens = queries.shape
    all_heads, part, _ = values.shape
    n_seq, n_val = lax.axis_size("seq"), lax.axis_size("val")
    nz = n_seq // NX
    blocks = tokens // W
    ev = part * n_val
    vm = pltpu.VMEM
    dma = pltpu.SemaphoreType.DMA
    row = (heads, blocks, 8, W)

    def matrix_scratch():
        return [
            vm((heads, blocks, FR, ev), F32),
            vm((NX, heads, QR, ev), BF16),
            vm((NX, heads, QR, ev), BF16),
            vm((heads, QR, ev), BF16),
            vm((nz, heads, QR, ev), BF16),
            vm((heads, QR, ev), F32),
            vm((NX, heads, QR, ev), BF16),
            vm((NX, heads, QR, ev), BF16),
        ]

    def vector_scratch():
        return [
            vm((8, FR), F32),
            vm((NX, 8, FR), F32),
            vm((8, FR), F32),
            vm((nz, 8, FR), F32),
            vm((8, FR), F32),
        ]

    scratch = [
        vm(queries.shape, BF16),
        vm((heads, width, W + tokens), BF16),
        vm((heads, ev, W + tokens), BF16),
        vm((heads, W + tokens, ev), BF16),
        vm((heads, ev, tokens), BF16),
        vm((heads, FR, tokens), BF16),
        vm((heads, FR, tokens), BF16),
        vm((heads, blocks, 2, 3 * CH, CH), BF16),
        vm((heads, blocks, 2, 2 * CH, CH), BF16),
        vm((heads, blocks, 2, 2 * CH, CH), BF16),
        vm((heads, ev, tokens), F32),
        vm((heads, ev, tokens), F32),
        vm((heads, width, tokens), F32),
        vm(row, F32),
        vm(row, F32),
        vm(row, F32),
        vm(row, F32),
        vm((heads, ev, tokens), BF16),
        vm((heads, width, tokens), F32),
        vm((heads, width, W + tokens), F32),
        vm((heads, ev, tokens), F32),
        vm((heads, ev, tokens), BF16),
        vm((heads, ev, tokens), BF16),
        vm((heads, blocks, 8, FR), F32),
        *vector_scratch(),
        vm((heads, blocks, FR, 128), F32),
        vm((heads, blocks, 8, FR), F32),
        *vector_scratch(),
        *matrix_scratch(),
        *matrix_scratch(),
        vm((heads, width, W), BF16),
        vm((heads, ev, W), BF16),
        vm((heads, width, W), BF16),
        vm((heads, ev, W), BF16),
        *[dma((blocks, n_val)) for _ in range(8)],
        *[dma((2,)), dma((blocks,)), dma((blocks,)), dma((blocks,)), dma((blocks,))],
        *[dma((2,)) for _ in range(4)],
        *[dma((NX,)), dma((NX,)), dma((nz,)), dma((nz,))] * 2,
        *[dma((NX,)), dma((NX,)), dma((nz,)), dma((nz,)), dma((NX,)), dma((NX,))] * 2,
    ]
    vmem = pl.BlockSpec(memory_space=pltpu.VMEM)
    hbm = pl.BlockSpec(memory_space=pl.ANY)
    outs = pl.pallas_call(
        functools.partial(kernel, n_seq, n_val),
        out_shape=(
            jax.ShapeDtypeStruct(values.shape, BF16),
            jax.ShapeDtypeStruct(queries.shape, F32),
            jax.ShapeDtypeStruct(keys.shape, F32),
            jax.ShapeDtypeStruct(values.shape, BF16),
        ),
        in_specs=[hbm, hbm, hbm, hbm],
        out_specs=(hbm, vmem, vmem, hbm),
        scratch_shapes=scratch,
        compiler_params=pltpu.CompilerParams(
            collective_id=0, has_side_effects=True, vmem_limit_bytes=56 << 20
        ),
        name="based_layer",
    )(queries, keys, values, out_grad)
    return pl.pallas_call(
        hand_on,
        out_shape=tuple(jax.ShapeDtypeStruct(o.shape, o.dtype) for o in outs),
        in_specs=[hbm] * len(outs),
        out_specs=(hbm,) * len(outs),
        scratch_shapes=[*[vm(o.shape, o.dtype) for o in outs], dma((2, len(outs)))],
        name="hand_on",
    )(*outs)


def solution(mesh):
    in_specs = (
        P("val", None, "seq"),
        P("val", None, "seq"),
        P(None, "val", "seq"),
        P(None, "val", "seq"),
    )
    out_specs = (
        P(None, "val", "seq"),
        P("val", None, "seq"),
        P("val", None, "seq"),
        P(None, "val", "seq"),
    )
    return jax.shard_map(local, mesh=mesh, in_specs=in_specs, out_specs=out_specs, check_vma=False)
```

```python
import functools

import jax
import jax.numpy as jnp
from jax import lax
from jax.experimental import pallas as pl
from jax.experimental.pallas import tpu as pltpu
from jax.sharding import PartitionSpec as P

W = 512
CH = 256
NX = 4
FR = 192
QR = FR // NX
LIN = 144
ROOT_HALF = 0.7071067811865476
NEG_LARGE = -1e30
MESH = pl.DeviceIdType.MESH
F32 = jnp.float32
BF16 = jnp.bfloat16


def dot(a, b, ca, cb):
    return lax.dot_general(a, b, (((ca,), (cb,)), ((), ())), preferred_element_type=F32)


def nn(a, b):
    return dot(a, b, 1, 0)


def nt(a, b):
    return dot(a, b, 1, 1)


def tn(a, b):
    return dot(a, b, 0, 0)


def turn_up(x, d):
    return jnp.concatenate([x[d:], x[:d]], axis=0) if d else x


def turn_down(x, d):
    return turn_up(x, 16 - d)


def split_rows(row):
    high = row.astype(BF16).astype(F32)
    low = row - high
    index = lax.broadcasted_iota(jnp.int32, (16, row.shape[1]), 0)
    return jnp.where(index == 0, high, jnp.where(index == 1, low, 0.0)).astype(BF16)


def when(condition, action):
    if condition is None:
        action()
    else:
        pl.when(condition)(action)


class Copy:
    def __init__(self, started, make, sends=None, takes=None):
        self.started, self.make, self.sends, self.takes = started, make, sends, takes
        self.waits = {"send", "recv"}

    def start(self):
        when(self.sends, lambda: self.make().start())
        self.started.append(self)

    def wait_recv(self):
        self.waits.discard("recv")
        when(self.takes, lambda: self.make().wait_recv())

    def finish(self):
        if "recv" in self.waits:
            self.wait_recv()
        when(self.sends, lambda: self.make().wait_send())


class Batch:
    def __init__(self, started, copies, whole, sent, ssem, rsem):
        self.started, self.copies, self.whole, self.sent, self.ssem, self.rsem = started, copies, whole, sent, ssem, rsem
        self.waiting = True

    def start(self):
        for c in self.copies:
            c.start()
        self.started.append(self)

    def wait_recv(self):
        self.waiting = False
        pltpu.make_async_copy(self.whole, self.whole, self.rsem).wait()

    def finish(self):
        if self.waiting:
            self.wait_recv()
        pltpu.make_async_copy(self.sent, self.sent, self.ssem).wait()


def pair_weights(columns):
    row = lax.broadcasted_iota(jnp.int32, (FR, columns), 0)
    return jnp.where(jnp.logical_and(row >= 16, row < 128), 2.0, 1.0)


def kernel(
    n_seq,
    n_val,
    q_hbm,
    k_hbm,
    v_hbm,
    g_hbm,
    mixed_out,
    dq_out,
    dk_out,
    dv_out,
    q_ref,
    kx,
    vx,
    vt,
    gx,
    fq,
    fk,
    es,
    cs,
    ts,
    num,
    win,
    kc,
    deni,
    rden,
    dd,
    dl,
    dn,
    dqa,
    dka,
    dva,
    mix,
    dvb,
    nrow,
    nsend,
    nxbuf,
    ntot,
    nzbuf,
    npre,
    ncol,
    drow,
    dsend,
    dxbuf,
    dtot,
    dzbuf,
    dsuf,
    s_blk,
    s_send,
    s_x,
    s_tot,
    s_z,
    s_acc,
    s_out,
    s_pre,
    u_blk,
    u_send,
    u_x,
    u_tot,
    u_z,
    u_acc,
    u_out,
    u_pre,
    hk_send,
    hv_send,
    hk_recv,
    hv_recv,
    va_s,
    va_r,
    ga_s,
    ga_r,
    mo_s,
    mo_r,
    do_s,
    do_r,
    loc,
    kh,
    vh,
    gkh,
    gvh,
    nxs,
    nxr,
    nzs,
    nzr,
    dxs,
    dxr,
    dzs,
    dzr,
    sxs,
    sxr,
    szs,
    szr,
    sos,
    sor,
    uxs,
    uxr,
    uzs,
    uzr,
    uos,
    uor,
):
    heads = q_ref.shape[0]
    tokens = q_ref.shape[2]
    blocks = tokens // W
    part = v_hbm.shape[1]
    nz = n_seq // NX
    seq = lax.axis_index("seq")
    val = lax.axis_index("val")
    z = seq // NX
    x = lax.rem(seq, NX)
    first = seq == 0
    last = seq == n_seq - 1
    after = lax.rem(seq + 1, n_seq)
    ahead = lax.rem(seq + n_seq - 1, n_seq)

    started = []

    def bare(src, dst, ssem, rsem, s, v):
        return pltpu.make_async_remote_copy(
            src_ref=src, dst_ref=dst, send_sem=ssem, recv_sem=rsem, device_id=(s, v), device_id_type=MESH
        )

    def remote(src, dst, ssem, rsem, s, v, sends=None, takes=None):
        return Copy(started, lambda: bare(src, dst, ssem, rsem, s, v), sends, takes)

    def drain():
        for c in started:
            c.finish()

    def val_peer(d):
        return lax.rem(val + d, n_val)

    def x_peer(d):
        return z * NX + lax.rem(x + d, NX)

    k_load = pltpu.make_async_copy(k_hbm, kx.at[:, :, pl.ds(W, tokens)], loc.at[0])
    q_load = pltpu.make_async_copy(q_hbm, q_ref, loc.at[1])
    k_load.start()
    q_load.start()
    barrier = pltpu.get_barrier_semaphore()

    def greet(s, v):
        pl.semaphore_signal(barrier, inc=1, device_id=(s, v), device_id_type=MESH)

    for d in range(1, n_val):
        greet(seq, val_peer(d))
    for d in range(1, NX):
        greet(x_peer(d), val)
    for d in range(1, nz):
        greet(lax.rem(z + d, nz) * NX + x, val)
    greet(after, val)
    greet(ahead, val)

    @pl.when(first)
    def _():
        kx[:, :, :W] = jnp.zeros((heads, 16, W), BF16)
        vx[:, :, :W] = jnp.zeros((heads, 128, W), BF16)

    k_load.wait()
    q_load.wait()
    pl.semaphore_wait(barrier, (n_val - 1) + (NX - 1) + (nz - 1) + 2)

    mine = pl.ds(pl.multiple_of(val * part, part), part)
    my_heads = pl.ds(val * heads, heads)

    def gather_copies(src, dst, off, ssem, rsem, b):
        copies = []
        span, to = pl.ds(b * W, W), pl.ds(off + b * W, W)
        for d in range(1, n_val):
            peer = val_peer(d)
            theirs = pl.ds(peer * heads, heads)
            copies.append(bare(src.at[theirs, :, span], dst.at[:, mine, to], ssem.at[b], rsem.at[b], seq, peer))
        copies.append(pltpu.make_async_copy(src.at[my_heads, :, span], dst.at[:, mine, to], rsem.at[b]))
        sent = dst.at[:, pl.ds(0, part * (n_val - 1)), to]
        return Batch(started, copies, dst.at[:, :, to], sent, ssem.at[b], rsem.at[b])

    v_copies = [gather_copies(v_hbm, vx, W, va_s, va_r, b) for b in range(blocks)]
    g_copies = [gather_copies(g_hbm, gx, 0, ga_s, ga_r, b) for b in range(blocks)]
    inner, outer = jnp.logical_not(first), jnp.logical_not(last)
    key_halo = remote(
        kx.at[:, :, pl.ds(tokens, W)], kx.at[:, :, pl.ds(0, W)], kh.at[0], kh.at[1], after, val, outer, inner
    )
    value_halo = remote(
        vx.at[:, :, pl.ds(tokens, W)], vx.at[:, :, pl.ds(0, W)], vh.at[0], vh.at[1], after, val, outer, inner
    )
    key_back = remote(hk_send, hk_recv, gkh.at[0], gkh.at[1], ahead, val, inner, outer)
    value_back = remote(hv_send, hv_recv, gvh.at[0], gvh.at[1], ahead, val, inner, outer)
    v_copies[blocks - 1].start()
    key_halo.start()
    for b in range(blocks - 1):
        v_copies[b].start()

    const = jnp.where(lax.broadcasted_iota(jnp.int32, (FR - LIN - 16, tokens), 0) == 0, 1.0, 0.0).astype(BF16)
    row_id = lax.broadcasted_iota(jnp.int32, (CH, CH), 0)
    col_id = lax.broadcasted_iota(jnp.int32, (CH, CH), 1)
    weights = pair_weights(128)
    ones = jnp.ones((16, W), BF16)

    def build_features(src, off, dst):
        def one(h, carry):
            xs = src[h, :, off : off + tokens].astype(F32) * 0.5
            for d in range(9):
                dst[h, 16 * d : 16 * d + 16, :] = (xs * turn_up(xs, d) * ROOT_HALF).astype(BF16)
            dst[h, LIN : LIN + 16, :] = xs.astype(BF16)
            dst[h, LIN + 16 :, :] = const
            return carry

        lax.fori_loop(0, heads, one, 0)

    def x_batch(copies, buf, ssem, rsem):
        bulk = buf.at[pl.ds(0, NX - 1)]
        return Batch(started, copies, bulk, bulk, ssem.at[0], rsem.at[0])

    def vector_x(send, buf, ssem, rsem):
        buf[x] = send[...]
        copies = [bare(send, buf.at[x], ssem.at[0], rsem.at[0], x_peer(d), val) for d in range(1, NX)]
        return x_batch(copies, buf, ssem, rsem)

    def scores(h, b):
        mask = row_id <= col_id
        for half in range(2):
            t0 = b * W + half * CH
            qs = (q_ref[h, :, t0 : t0 + CH].astype(F32) * 0.25).astype(BF16)
            s = tn(kx[h, :, t0 : t0 + 3 * CH], qs)
            s_old, s_mid, s_own = s[:CH], s[CH : 2 * CH], s[2 * CH :]
            w_mid = s_mid
            if b == 0:
                gone = jnp.where(first, NEG_LARGE, 0.0)
                s_old = s_old + gone
                if half == 0:
                    w_mid = s_mid + gone
            s_diag = jnp.where(mask, s_own, s_old)
            top = jnp.maximum(
                jnp.max(s_diag, axis=0, keepdims=True), jnp.max(w_mid, axis=0, keepdims=True)
            )
            e_diag = jnp.exp(s_diag - top)
            e_mid = jnp.exp(w_mid - top)
            sums = jnp.sum(e_diag, axis=0, keepdims=True) + jnp.sum(e_mid, axis=0, keepdims=True)
            scale = 1.0 / sums
            p_diag = e_diag * scale
            es[h, b, half, :CH] = jnp.where(mask, 0.0, p_diag).astype(BF16)
            es[h, b, half, CH : 2 * CH] = (e_mid * scale).astype(BF16)
            es[h, b, half, 2 * CH :] = jnp.where(mask, p_diag, 0.0).astype(BF16)
            c_own = 1.0 + s_own
            t_own = jnp.where(mask, 0.5 * (c_own * c_own) + 0.5, 0.0)
            den = jnp.sum(t_own, axis=0, keepdims=True)
            cs[h, b, half, CH:] = jnp.where(mask, c_own, 0.0).astype(BF16)
            ts[h, b, half, CH:] = t_own.astype(BF16)
            if half == 1:
                c_mid = 1.0 + s_mid
                t_mid = 0.5 * (c_mid * c_mid) + 0.5
                den = den + jnp.sum(t_mid, axis=0, keepdims=True)
                cs[h, b, half, :CH] = c_mid.astype(BF16)
                ts[h, b, half, :CH] = t_mid.astype(BF16)
            deni[h, b, :1, half * CH : (half + 1) * CH] = den

    def each_head(body):
        def one(h, carry):
            body(h)
            return carry

        lax.fori_loop(0, heads, one, 0)

    def along_z(tot, buf, ssem, rsem, forward):
        copies = []
        for d in range(1, nz):
            to = z + d if forward else z - d
            up, down = z + d < nz, z >= d
            sends, takes = (up, down) if forward else (down, up)
            copies.append(remote(tot, buf.at[d], ssem.at[d - 1], rsem.at[d - 1], to * NX + x, val, sends, takes))
            copies[-1].start()
        return copies

    def vector_total(copies, buf, tot):
        copies.wait_recv()
        total = buf[0]
        for i in range(1, NX):
            total = total + buf[i]
        tot[...] = total

    def vector_end(xbuf, copies, zbuf, out, forward):
        acc = jnp.zeros((8, FR), F32)
        for i in range(NX):
            taken = (i < x) if forward else (i > x)
            acc = acc + jnp.where(taken, xbuf[i], 0.0)
        out[...] = acc
        add_arrivals(copies, zbuf, out)

    def add_arrivals(copies, zbuf, out):
        for i, c in enumerate(copies):
            c.wait_recv()

            def add():
                out[...] += zbuf[i + 1].astype(F32)

            when(c.takes, add)

    def as_column(row):
        return jnp.transpose(jnp.broadcast_to(row, (128, row.shape[1])))

    def matrix_send(h, total, send):
        low = total.astype(BF16)
        for i in range(NX):
            send[i, h] = low[i * QR : (i + 1) * QR]

    def matrix_x(send, buf, ssem, rsem):
        copies = [
            bare(send.at[lax.rem(x + d, NX)], buf.at[x], ssem.at[0], rsem.at[0], x_peer(d), val)
            for d in range(1, NX)
        ]
        return x_batch(copies, buf, ssem, rsem)

    def matrix_total(copies, send, buf, tot):
        copies.wait_recv()
        total = buf[0].astype(F32)
        for i in range(1, NX):
            total = total + buf[i].astype(F32)
        tot[...] = total.astype(BF16)

    def matrix_end(buf, copies, zbuf, acc, out, forward):
        acc[...] = jnp.zeros(acc.shape, F32)
        add_arrivals(copies, zbuf, acc)
        running = acc[...]
        order = range(NX) if forward else range(NX - 1, -1, -1)
        for i in order:
            out[i] = running.astype(BF16)
            running = running + buf[i].astype(F32)

    def matrix_out(out, pre, ssem, rsem):
        pre[x] = out[x]
        copies = [
            bare(out.at[lax.rem(x + d, NX)], pre.at[x], ssem.at[0], rsem.at[0], x_peer(d), val)
            for d in range(1, NX)
        ]
        return x_batch(copies, pre, ssem, rsem)

    def scores_values(h):
        for b in range(blocks):
            for half in range(2):
                lo = 0 if half else CH
                own = slice(W + b * W, W + b * W + (half + 1) * CH)
                cols = slice(b * W + half * CH, b * W + (half + 1) * CH)
                num[h, :, cols] = nn(vx[h, :, own], ts[h, b, half, lo:])
                kc[h, :, cols] = nn(kx[h, :, own], cs[h, b, half, lo:])

    def windows(h, b):
        for half in range(2):
            t0 = b * W + half * CH
            win[h, :, t0 : t0 + CH] = nn(vx[h, :, t0 : t0 + 3 * CH], es[h, b, half])

    def scale_grads(h):
        for b in range(blocks):
            cols = slice(b * W, (b + 1) * W)
            wide = gx[h, :, cols].astype(F32)
            dn[h, :, cols] = (wide * rden[h, b, :1]).astype(BF16)

    def halo_values(h):
        for i in range(2):
            total = nt(gx[h, :, :CH], es[h, 0, 0, i * CH : (i + 1) * CH])
            if i == 1:
                total = total + nt(gx[h, :, CH:W], es[h, 0, 1, :CH])
            hv_send[h, :, i * CH : (i + 1) * CH] = total.astype(BF16)

    def turn_values(h, lo):
        for i in range(lo // CH, (vx.shape[2] if lo else W) // CH):
            vt[h, i * CH : (i + 1) * CH] = jnp.transpose(vx[h, :, i * CH : (i + 1) * CH].astype(F32)).astype(BF16)

    def deltas(h):
        for b in range(blocks):
            cols = slice(b * W, (b + 1) * W)
            dl[h, b, :1] = jnp.sum(gx[h, :, cols].astype(F32) * win[h, :, cols], axis=0, keepdims=True)

    def whole(pre, h):
        return jnp.concatenate([pre[i, h].astype(F32) for i in range(NX)], axis=0)

    def fold(grad, rows):
        xs = rows.astype(F32) * 0.5
        acc = 2.0 * (grad[:16] * xs + grad[128:144] * turn_up(xs, 8))
        for d in range(1, 8):
            one = grad[16 * d : 16 * d + 16]
            acc = acc + one * turn_up(xs, d) + turn_down(one * xs, d)
        return 0.5 * grad[LIN : LIN + 16] + (0.5 * ROOT_HALF) * acc

    def forward_state(h, b):
        state = whole(s_pre, h)
        for i in range(b):
            state = state + s_blk[h, i]
        return (state * weights).astype(BF16)

    def scatter(src, dst, ssem, rsem, b):
        copies = []
        span = pl.ds(b * W, W)
        for d in range(1, n_val):
            peer = val_peer(d)
            rows = pl.ds(pl.multiple_of(peer * part, part), part)
            copies.append(bare(src.at[:, rows, span], dst.at[my_heads, :, span], ssem.at[b], rsem.at[b], seq, peer))
        copies.append(pltpu.make_async_copy(src.at[:, mine, span], dst.at[my_heads, :, span], rsem.at[b]))
        sent = src.at[:, pl.ds(0, part * (n_val - 1)), span]
        return Batch(started, copies, dst.at[:, :, span], sent, ssem.at[b], rsem.at[b])

    def query_end(h):
        for b in range(blocks):
            cols = slice(b * W, (b + 1) * W)
            d_row = dd[h, b, :1]
            grad = nn(forward_state(h, b), dn[h, :, cols])
            grad = grad + jnp.concatenate([ncol[h, b]] * (W // 128), axis=1) * d_row
            local = dqa[h, :, cols] + d_row * kc[h, :, cols]
            dq_out[h, :, cols] = 0.25 * local + fold(grad, q_ref[h, :, cols])
            qd = (q_ref[h, :, cols].astype(F32) * d_row).astype(BF16)
            for half in range(2):
                lo = 0 if half else CH
                own = slice(W + b * W, W + b * W + (half + 1) * CH)
                dka[h, :, own] += nt(qd[:, half * CH : (half + 1) * CH], cs[h, b, half, lo:])

    def suffix_of(h, b):
        state = whole(u_pre, h)
        for i in range(b + 1, blocks):
            state = state + u_blk[h, i]
        return (state * weights).astype(BF16)

    def value_end(h, b):
        cols = slice(b * W, (b + 1) * W)
        inter = tn(suffix_of(h, b), fk[h, :, cols])
        dvb[h, :, cols] = (dva[h, :, cols] + inter).astype(BF16)

    def norm_rows():
        for h in range(heads):
            total = jnp.zeros((1, FR), F32)
            for b in range(blocks):
                row = nt(ones, fk[h, :, b * W : (b + 1) * W])[:1]
                nrow[h, b, :1] = row
                total = total + row
            nsend[h : h + 1, :] = total
        nsend[heads:, :] = jnp.zeros((8 - heads, FR), F32)

    def denominators():
        for h in range(heads):
            row = npre[h : h + 1, :]
            for b in range(blocks):
                column = as_column(row) * weights
                ncol[h, b] = column
                for i in range(W // 128):
                    lanes = slice(b * W + i * 128, b * W + (i + 1) * 128)
                    inter = jnp.sum(fq[h, :, lanes].astype(F32) * column, axis=0, keepdims=True)
                    here = slice(i * 128, (i + 1) * 128)
                    rden[h, b, :1, here] = 1.0 / (deni[h, b, :1, here] + inter)
                row = row + nrow[h, b, :1]

    def state_terms(feats, rows, off, blk, send):
        for h in range(heads):
            total = None
            for b in range(blocks):
                term = nt(feats[h, :, b * W : (b + 1) * W], rows[h, :, off + b * W : off + (b + 1) * W])
                blk[h, b] = term
                total = term if total is None else total + term
            matrix_send(h, total, send)

    def value_local(h, b):
        base = b * W
        total = nt(gx[h, :, base : base + CH], es[h, b, 0, 2 * CH :])
        total = total + nt(gx[h, :, base + CH : base + W], es[h, b, 1, CH : 2 * CH])
        total = total + nt(dn[h, :, base : base + CH], ts[h, b, 0, CH:])
        total = total + nt(dn[h, :, base + CH : base + W], ts[h, b, 1, :CH])
        last_half = nt(gx[h, :, base + CH : base + W], es[h, b, 1, 2 * CH :])
        last_half = last_half + nt(dn[h, :, base + CH : base + W], ts[h, b, 1, CH:])
        if b + 1 < blocks:
            after_base = base + W
            total = total + nt(gx[h, :, after_base : after_base + CH], es[h, b + 1, 0, :CH])
            last_half = last_half + nt(gx[h, :, after_base : after_base + CH], es[h, b + 1, 0, CH : 2 * CH])
            last_half = last_half + nt(gx[h, :, after_base + CH : after_base + W], es[h, b + 1, 1, :CH])
        dva[h, :, base : base + CH] = total
        dva[h, :, base + CH : base + W] = last_half

    def score_grads(h, b):
        for half in range(2):
            lo = 0 if half else CH
            t0 = b * W + half * CH
            cols = slice(t0, t0 + CH)
            keys = slice(t0, t0 + 3 * CH)
            own = slice(W + b * W, W + b * W + (half + 1) * CH)
            count = (half + 1) * CH
            mixing = nn(vt[h, keys], gx[h, :, cols])
            mixing_dn = nn(vt[h, own], dn[h, :, cols])
            gs = es[h, b, half].astype(F32) * (mixing - dl[h, b, :1, half * CH : (half + 1) * CH])
            taylor = cs[h, b, half, lo:].astype(F32) * mixing_dn
            gs = jnp.concatenate([gs[: 3 * CH - count], gs[3 * CH - count :] + taylor], axis=0).astype(BF16)
            dqa[h, :, cols] = nn(kx[h, :, keys], gs)
            dka[h, :, keys] += nt(q_ref[h, :, cols], gs)

    def linear_out(h):
        for b in range(blocks):
            cols = slice(b * W, (b + 1) * W)
            lin = (num[h, :, cols] + tn(forward_state(h, b), fq[h, :, cols])) * rden[h, b, :1]
            num[h, :, cols] = lin
            mix[h, :, cols] = (lin + win[h, :, cols]).astype(BF16)

    def den_grads(h):
        for b in range(blocks):
            cols = slice(b * W, (b + 1) * W)
            d_row = -jnp.sum(gx[h, :, cols].astype(F32) * num[h, :, cols], axis=0, keepdims=True) * rden[h, b, :1]
            dd[h, b, :1] = d_row
            drow[h, b, :1] = jnp.sum(nt(split_rows(d_row), fq[h, :, cols]), axis=0, keepdims=True)

    def den_rows():
        for h in range(heads):
            total = drow[h, 0, :1]
            for b in range(1, blocks):
                total = total + drow[h, b, :1]
            dsend[h : h + 1, :] = total
        dsend[heads:, :] = jnp.zeros((8 - heads, FR), F32)

    def key_end(h):
        row = dsuf[h : h + 1, :]
        for b in range(blocks - 1, -1, -1):
            cols = slice(b * W, (b + 1) * W)
            own = slice(W + b * W, W + (b + 1) * W)
            column = as_column(row) * weights
            grad = nn(suffix_of(h, b), vx[h, :, own])
            grad = grad + jnp.concatenate([column] * (W // 128), axis=1)
            dk_out[h, :, cols] = 0.25 * dka[h, :, own] + fold(grad, kx[h, :, own])
            row = row + drow[h, b, :1]

    build_features(kx, W, fk)
    norm_rows()
    n_1 = vector_x(nsend, nxbuf, nxs, nxr)
    n_1.start()
    build_features(q_ref, 0, fq)
    for b in range(1, blocks):
        each_head(functools.partial(lambda h, b: scores(h, b), b=b))
    vector_total(n_1, nxbuf, ntot)
    n_2 = along_z(ntot, nzbuf, nzs, nzr, True)
    key_halo.wait_recv()
    each_head(lambda h: scores(h, 0))
    v_copies[blocks - 1].wait_recv()
    value_halo.start()
    g_copies[0].start()
    vector_end(nxbuf, n_2, nzbuf, npre, True)
    denominators()
    for b in range(blocks - 1):
        v_copies[b].wait_recv()
    for b in range(1, blocks):
        g_copies[b].start()

    state_terms(fk, vx, W, s_blk, s_send)
    s_x[x] = s_send[x]
    s_1 = matrix_x(s_send, s_x, sxs, sxr)
    s_1.start()
    each_head(scores_values)
    for b in range(1, blocks):
        each_head(functools.partial(lambda h, b: windows(h, b), b=b))
    each_head(functools.partial(turn_values, lo=W))
    matrix_total(s_1, s_send, s_x, s_tot)
    s_2 = along_z(s_tot, s_z, szs, szr, True)
    value_halo.wait_recv()
    each_head(lambda h: windows(h, 0))

    g_copies[0].wait_recv()
    for b in range(1, blocks):
        g_copies[b].wait_recv()
    each_head(scale_grads)
    state_terms(fq, dn, 0, u_blk, u_send)
    u_x[x] = u_send[x]
    u_1 = matrix_x(u_send, u_x, uxs, uxr)
    u_1.start()
    each_head(halo_values)
    value_back.start()
    matrix_end(s_x, s_2, s_z, s_acc, s_out, True)
    s_3 = matrix_out(s_out, s_pre, sos, sor)
    s_3.start()
    for b in range(blocks):
        each_head(functools.partial(lambda h, b: value_local(h, b), b=b))
    matrix_total(u_1, u_send, u_x, u_tot)
    u_2 = along_z(u_tot, u_z, uzs, uzr, False)
    s_3.wait_recv()
    each_head(linear_out)
    for b in range(blocks):
        scatter(mix, mixed_out, mo_s, mo_r, b).start()
    each_head(den_grads)
    den_rows()
    d_1 = vector_x(dsend, dxbuf, dxs, dxr)
    d_1.start()
    each_head(functools.partial(turn_values, lo=0))
    each_head(deltas)
    dka[...] = jnp.zeros(dka.shape, F32)
    matrix_end(u_x, u_2, u_z, u_acc, u_out, False)
    u_3 = matrix_out(u_out, u_pre, uos, uor)
    u_3.start()
    each_head(lambda h: score_grads(h, 0))
    hk_send[...] = (0.25 * dka[:, :, :W]).astype(BF16)
    key_back.start()
    vector_total(d_1, dxbuf, dtot)
    d_2 = along_z(dtot, dzbuf, dzs, dzr, False)
    value_back.wait_recv()

    @pl.when(outer)
    def _():
        dva[:, :, tokens - W :] += hv_recv[...].astype(F32)

    u_3.wait_recv()
    for b in range(blocks):
        each_head(functools.partial(lambda h, b: value_end(h, b), b=b))
        scatter(dvb, dv_out, do_s, do_r, b).start()

    for b in range(1, blocks):
        each_head(functools.partial(lambda h, b: score_grads(h, b), b=b))
    each_head(query_end)
    key_back.wait_recv()

    @pl.when(outer)
    def _():
        dka[:, :, tokens:] += 4.0 * hk_recv[...].astype(F32)

    vector_end(dxbuf, d_2, dzbuf, dsuf, False)
    for h in range(heads):
        key_end(h)
    drain()


def hand_on(*refs):
    count = len(refs) // 3
    take_in, give_out = refs[-1].at[0], refs[-1].at[1]
    loads, stores = [], []
    for i in range(count):
        source, target, held = refs[i], refs[count + i], refs[2 * count + i]
        loads.append(pltpu.make_async_copy(source, held, take_in.at[i]))
        stores.append(pltpu.make_async_copy(held, target, give_out.at[i]))
    for c in loads:
        c.start()
    for load, store in zip(loads, stores):
        load.wait()
        store.start()
    for c in stores:
        c.wait()


def local(queries, keys, values, out_grad):
    heads, width, tokens = queries.shape
    all_heads, part, _ = values.shape
    n_seq, n_val = lax.axis_size("seq"), lax.axis_size("val")
    nz = n_seq // NX
    blocks = tokens // W
    ev = part * n_val
    vm = pltpu.VMEM
    dma = pltpu.SemaphoreType.DMA
    row = (heads, blocks, 8, W)

    def matrix_scratch():
        return [
            vm((heads, blocks, FR, ev), F32),
            vm((NX, heads, QR, ev), BF16),
            vm((NX, heads, QR, ev), BF16),
            vm((heads, QR, ev), BF16),
            vm((nz, heads, QR, ev), BF16),
            vm((heads, QR, ev), F32),
            vm((NX, heads, QR, ev), BF16),
            vm((NX, heads, QR, ev), BF16),
        ]

    def vector_scratch():
        return [
            vm((8, FR), F32),
            vm((NX, 8, FR), F32),
            vm((8, FR), F32),
            vm((nz, 8, FR), F32),
            vm((8, FR), F32),
        ]

    scratch = [
        vm(queries.shape, BF16),
        vm((heads, width, W + tokens), BF16),
        vm((heads, ev, W + tokens), BF16),
        vm((heads, W + tokens, ev), BF16),
        vm((heads, ev, tokens), BF16),
        vm((heads, FR, tokens), BF16),
        vm((heads, FR, tokens), BF16),
        vm((heads, blocks, 2, 3 * CH, CH), BF16),
        vm((heads, blocks, 2, 2 * CH, CH), BF16),
        vm((heads, blocks, 2, 2 * CH, CH), BF16),
        vm((heads, ev, tokens), F32),
        vm((heads, ev, tokens), F32),
        vm((heads, width, tokens), F32),
        vm(row, F32),
        vm(row, F32),
        vm(row, F32),
        vm(row, F32),
        vm((heads, ev, tokens), BF16),
        vm((heads, width, tokens), F32),
        vm((heads, width, W + tokens), F32),
        vm((heads, ev, tokens), F32),
        vm((heads, ev, tokens), BF16),
        vm((heads, ev, tokens), BF16),
        vm((heads, blocks, 8, FR), F32),
        *vector_scratch(),
        vm((heads, blocks, FR, 128), F32),
        vm((heads, blocks, 8, FR), F32),
        *vector_scratch(),
        *matrix_scratch(),
        *matrix_scratch(),
        vm((heads, width, W), BF16),
        vm((heads, ev, W), BF16),
        vm((heads, width, W), BF16),
        vm((heads, ev, W), BF16),
        *[dma((blocks,)) for _ in range(8)],
        *[dma((2,)) for _ in range(5)],
        *[dma((1,)), dma((1,)), dma((nz - 1,)), dma((nz - 1,))] * 2,
        *[dma((1,)), dma((1,)), dma((nz - 1,)), dma((nz - 1,)), dma((1,)), dma((1,))] * 2,
    ]
    vmem = pl.BlockSpec(memory_space=pltpu.VMEM)
    hbm = pl.BlockSpec(memory_space=pl.ANY)
    outs = pl.pallas_call(
        functools.partial(kernel, n_seq, n_val),
        out_shape=(
            jax.ShapeDtypeStruct(values.shape, BF16),
            jax.ShapeDtypeStruct(queries.shape, F32),
            jax.ShapeDtypeStruct(keys.shape, F32),
            jax.ShapeDtypeStruct(values.shape, BF16),
        ),
        in_specs=[hbm, hbm, hbm, hbm],
        out_specs=(hbm, vmem, vmem, hbm),
        scratch_shapes=scratch,
        compiler_params=pltpu.CompilerParams(
            collective_id=0, has_side_effects=True, vmem_limit_bytes=56 << 20
        ),
        name="based_layer",
    )(queries, keys, values, out_grad)
    return pl.pallas_call(
        hand_on,
        out_shape=tuple(jax.ShapeDtypeStruct(o.shape, o.dtype) for o in outs),
        in_specs=[hbm] * len(outs),
        out_specs=(hbm,) * len(outs),
        scratch_shapes=[*[vm(o.shape, o.dtype) for o in outs], dma((2, len(outs)))],
        name="hand_on",
    )(*outs)


def solution(mesh):
    in_specs = (
        P("val", None, "seq"),
        P("val", None, "seq"),
        P(None, "val", "seq"),
        P(None, "val", "seq"),
    )
    out_specs = (
        P(None, "val", "seq"),
        P("val", None, "seq"),
        P("val", None, "seq"),
        P(None, "val", "seq"),
    )
    return jax.shard_map(local, mesh=mesh, in_specs=in_specs, out_specs=out_specs, check_vma=False)
```

```python
import functools

import jax
import jax.numpy as jnp
from jax import lax
from jax.experimental import pallas as pl
from jax.experimental.pallas import tpu as pltpu
from jax.sharding import PartitionSpec as P

W = 512
CH = 256
NX = 4
FR = 192
QR = FR // NX
LIN = 144
ROOT_HALF = 0.7071067811865476
NEG_LARGE = -1e30
MESH = pl.DeviceIdType.MESH
F32 = jnp.float32
BF16 = jnp.bfloat16


def dot(a, b, ca, cb):
    return lax.dot_general(a, b, (((ca,), (cb,)), ((), ())), preferred_element_type=F32)


def nn(a, b):
    return dot(a, b, 1, 0)


def nt(a, b):
    return dot(a, b, 1, 1)


def tn(a, b):
    return dot(a, b, 0, 0)


def turn_up(x, d):
    return jnp.concatenate([x[d:], x[:d]], axis=0) if d else x


def turn_down(x, d):
    return turn_up(x, 16 - d)


def split_rows(row):
    high = row.astype(BF16).astype(F32)
    low = row - high
    index = lax.broadcasted_iota(jnp.int32, (16, row.shape[1]), 0)
    return jnp.where(index == 0, high, jnp.where(index == 1, low, 0.0)).astype(BF16)


def when(condition, action):
    if condition is None:
        action()
    else:
        pl.when(condition)(action)


class Copy:
    def __init__(self, started, make, sends=None, takes=None):
        self.started, self.make, self.sends, self.takes = started, make, sends, takes
        self.waits = {"send", "recv"}

    def start(self):
        when(self.sends, lambda: self.make().start())
        self.started.append(self)

    def wait_recv(self):
        self.waits.discard("recv")
        when(self.takes, lambda: self.make().wait_recv())

    def finish(self):
        if "recv" in self.waits:
            self.wait_recv()
        when(self.sends, lambda: self.make().wait_send())


class Batch:
    def __init__(self, started, copies, whole, sent, ssem, rsem):
        self.started, self.copies, self.whole, self.sent, self.ssem, self.rsem = started, copies, whole, sent, ssem, rsem
        self.waiting = True

    def start(self):
        for c in self.copies:
            c.start()
        self.started.append(self)

    def wait_recv(self):
        self.waiting = False
        pltpu.make_async_copy(self.whole, self.whole, self.rsem).wait()

    def finish(self):
        if self.waiting:
            self.wait_recv()
        pltpu.make_async_copy(self.sent, self.sent, self.ssem).wait()


def pair_weights(columns):
    row = lax.broadcasted_iota(jnp.int32, (FR, columns), 0)
    return jnp.where(jnp.logical_and(row >= 16, row < 128), 2.0, 1.0)


def kernel(
    n_seq,
    n_val,
    q_hbm,
    k_hbm,
    v_hbm,
    g_hbm,
    mixed_out,
    dq_out,
    dk_out,
    dv_out,
    q_ref,
    kx,
    vx,
    vt,
    gx,
    fq,
    fk,
    es,
    cs,
    ts,
    num,
    win,
    kc,
    deni,
    rden,
    dd,
    dl,
    dn,
    dqa,
    dka,
    dva,
    mix,
    dvb,
    nrow,
    nsend,
    nxbuf,
    ntot,
    nzbuf,
    npre,
    ncol,
    drow,
    dsend,
    dxbuf,
    dtot,
    dzbuf,
    dsuf,
    s_blk,
    s_send,
    s_x,
    s_tot,
    s_z,
    s_acc,
    s_out,
    s_pre,
    u_blk,
    u_send,
    u_x,
    u_tot,
    u_z,
    u_acc,
    u_out,
    u_pre,
    hk_send,
    hv_send,
    hk_recv,
    hv_recv,
    va_s,
    va_r,
    ga_s,
    ga_r,
    mo_s,
    mo_r,
    do_s,
    do_r,
    loc,
    kh,
    vh,
    gkh,
    gvh,
    nxs,
    nxr,
    nzs,
    nzr,
    dxs,
    dxr,
    dzs,
    dzr,
    sxs,
    sxr,
    szs,
    szr,
    sos,
    sor,
    uxs,
    uxr,
    uzs,
    uzr,
    uos,
    uor,
):
    heads = q_ref.shape[0]
    tokens = q_ref.shape[2]
    blocks = tokens // W
    part = v_hbm.shape[1]
    nz = n_seq // NX
    seq = lax.axis_index("seq")
    val = lax.axis_index("val")
    z = seq // NX
    x = lax.rem(seq, NX)
    first = seq == 0
    last = seq == n_seq - 1
    after = lax.rem(seq + 1, n_seq)
    ahead = lax.rem(seq + n_seq - 1, n_seq)

    started = []

    def bare(src, dst, ssem, rsem, s, v):
        return pltpu.make_async_remote_copy(
            src_ref=src, dst_ref=dst, send_sem=ssem, recv_sem=rsem, device_id=(s, v), device_id_type=MESH
        )

    def remote(src, dst, ssem, rsem, s, v, sends=None, takes=None):
        return Copy(started, lambda: bare(src, dst, ssem, rsem, s, v), sends, takes)

    def drain():
        for c in started:
            c.finish()

    def val_peer(d):
        return lax.rem(val + d, n_val)

    def x_peer(d):
        return z * NX + lax.rem(x + d, NX)

    k_load = pltpu.make_async_copy(k_hbm, kx.at[:, :, pl.ds(W, tokens)], loc.at[0])
    q_load = pltpu.make_async_copy(q_hbm, q_ref, loc.at[1])
    k_load.start()
    q_load.start()
    barrier = pltpu.get_barrier_semaphore()

    def greet(s, v):
        pl.semaphore_signal(barrier, inc=1, device_id=(s, v), device_id_type=MESH)

    for d in range(1, n_val):
        greet(seq, val_peer(d))
    for d in range(1, NX):
        greet(x_peer(d), val)
    for d in range(1, nz):
        greet(lax.rem(z + d, nz) * NX + x, val)
    greet(after, val)
    greet(ahead, val)

    @pl.when(first)
    def _():
        kx[:, :, :W] = jnp.zeros((heads, 16, W), BF16)
        vx[:, :, :W] = jnp.zeros((heads, 128, W), BF16)

    pl.semaphore_wait(barrier, (n_val - 1) + (NX - 1) + (nz - 1) + 2)

    mine = pl.ds(pl.multiple_of(val * part, part), part)
    my_heads = pl.ds(val * heads, heads)

    def gather_copies(src, dst, off, ssem, rsem, b):
        copies = []
        span, to = pl.ds(b * W, W), pl.ds(off + b * W, W)
        for d in range(1, n_val):
            peer = val_peer(d)
            theirs = pl.ds(peer * heads, heads)
            copies.append(bare(src.at[theirs, :, span], dst.at[:, mine, to], ssem.at[b], rsem.at[b], seq, peer))
        copies.append(pltpu.make_async_copy(src.at[my_heads, :, span], dst.at[:, mine, to], rsem.at[b]))
        sent = dst.at[:, pl.ds(0, part * (n_val - 1)), to]
        return Batch(started, copies, dst.at[:, :, to], sent, ssem.at[b], rsem.at[b])

    v_copies = [gather_copies(v_hbm, vx, W, va_s, va_r, b) for b in range(blocks)]
    g_copies = [gather_copies(g_hbm, gx, 0, ga_s, ga_r, b) for b in range(blocks)]
    inner, outer = jnp.logical_not(first), jnp.logical_not(last)
    key_halo = remote(
        kx.at[:, :, pl.ds(tokens, W)], kx.at[:, :, pl.ds(0, W)], kh.at[0], kh.at[1], after, val, outer, inner
    )
    value_halo = remote(
        vx.at[:, :, pl.ds(tokens, W)], vx.at[:, :, pl.ds(0, W)], vh.at[0], vh.at[1], after, val, outer, inner
    )
    key_back = remote(hk_send, hk_recv, gkh.at[0], gkh.at[1], ahead, val, inner, outer)
    value_back = remote(hv_send, hv_recv, gvh.at[0], gvh.at[1], ahead, val, inner, outer)
    v_copies[blocks - 1].start()
    for b in range(blocks - 1):
        v_copies[b].start()
    k_load.wait()
    q_load.wait()
    key_halo.start()

    const = jnp.where(lax.broadcasted_iota(jnp.int32, (FR - LIN - 16, tokens), 0) == 0, 1.0, 0.0).astype(BF16)
    row_id = lax.broadcasted_iota(jnp.int32, (CH, CH), 0)
    col_id = lax.broadcasted_iota(jnp.int32, (CH, CH), 1)
    weights = pair_weights(128)
    ones = jnp.ones((16, W), BF16)

    def build_features(src, off, dst):
        def one(h, carry):
            xs = src[h, :, off : off + tokens].astype(F32) * 0.5
            for d in range(9):
                dst[h, 16 * d : 16 * d + 16, :] = (xs * turn_up(xs, d) * ROOT_HALF).astype(BF16)
            dst[h, LIN : LIN + 16, :] = xs.astype(BF16)
            dst[h, LIN + 16 :, :] = const
            return carry

        lax.fori_loop(0, heads, one, 0)

    def x_batch(copies, buf, ssem, rsem):
        bulk = buf.at[pl.ds(0, NX - 1)]
        return Batch(started, copies, bulk, bulk, ssem.at[0], rsem.at[0])

    def vector_x(send, buf, ssem, rsem):
        buf[x] = send[...]
        copies = [bare(send, buf.at[x], ssem.at[0], rsem.at[0], x_peer(d), val) for d in range(1, NX)]
        return x_batch(copies, buf, ssem, rsem)

    def scores(h, b):
        mask = row_id <= col_id
        for half in range(2):
            t0 = b * W + half * CH
            qs = (q_ref[h, :, t0 : t0 + CH].astype(F32) * 0.25).astype(BF16)
            s = tn(kx[h, :, t0 : t0 + 3 * CH], qs)
            s_old, s_mid, s_own = s[:CH], s[CH : 2 * CH], s[2 * CH :]
            w_mid = s_mid
            if b == 0:
                gone = jnp.where(first, NEG_LARGE, 0.0)
                s_old = s_old + gone
                if half == 0:
                    w_mid = s_mid + gone
            s_diag = jnp.where(mask, s_own, s_old)
            top = jnp.maximum(
                jnp.max(s_diag, axis=0, keepdims=True), jnp.max(w_mid, axis=0, keepdims=True)
            )
            e_diag = jnp.exp(s_diag - top)
            e_mid = jnp.exp(w_mid - top)
            sums = jnp.sum(e_diag, axis=0, keepdims=True) + jnp.sum(e_mid, axis=0, keepdims=True)
            scale = 1.0 / sums
            p_diag = e_diag * scale
            es[h, b, half, :CH] = jnp.where(mask, 0.0, p_diag).astype(BF16)
            es[h, b, half, CH : 2 * CH] = (e_mid * scale).astype(BF16)
            es[h, b, half, 2 * CH :] = jnp.where(mask, p_diag, 0.0).astype(BF16)
            c_own = 1.0 + s_own
            t_own = jnp.where(mask, 0.5 * (c_own * c_own) + 0.5, 0.0)
            den = jnp.sum(t_own, axis=0, keepdims=True)
            cs[h, b, half, CH:] = jnp.where(mask, c_own, 0.0).astype(BF16)
            ts[h, b, half, CH:] = t_own.astype(BF16)
            if half == 1:
                c_mid = 1.0 + s_mid
                t_mid = 0.5 * (c_mid * c_mid) + 0.5
                den = den + jnp.sum(t_mid, axis=0, keepdims=True)
                cs[h, b, half, :CH] = c_mid.astype(BF16)
                ts[h, b, half, :CH] = t_mid.astype(BF16)
            deni[h, b, :1, half * CH : (half + 1) * CH] = den

    def each_head(body):
        def one(h, carry):
            body(h)
            return carry

        lax.fori_loop(0, heads, one, 0)

    def along_z(tot, buf, ssem, rsem, forward):
        copies = []
        for d in range(1, nz):
            to = z + d if forward else z - d
            up, down = z + d < nz, z >= d
            sends, takes = (up, down) if forward else (down, up)
            copies.append(remote(tot, buf.at[d], ssem.at[d - 1], rsem.at[d - 1], to * NX + x, val, sends, takes))
            copies[-1].start()
        return copies

    def vector_total(copies, buf, tot):
        copies.wait_recv()
        total = buf[0]
        for i in range(1, NX):
            total = total + buf[i]
        tot[...] = total

    def vector_end(xbuf, copies, zbuf, out, forward):
        acc = jnp.zeros((8, FR), F32)
        for i in range(NX):
            taken = (i < x) if forward else (i > x)
            acc = acc + jnp.where(taken, xbuf[i], 0.0)
        out[...] = acc
        add_arrivals(copies, zbuf, out)

    def add_arrivals(copies, zbuf, out):
        for i, c in enumerate(copies):
            c.wait_recv()

            def add():
                out[...] += zbuf[i + 1].astype(F32)

            when(c.takes, add)

    def as_column(row):
        return jnp.transpose(jnp.broadcast_to(row, (128, row.shape[1])))

    def matrix_send(h, total, send):
        low = total.astype(BF16)
        for i in range(NX):
            send[i, h] = low[i * QR : (i + 1) * QR]

    def matrix_x(send, buf, ssem, rsem):
        copies = [
            bare(send.at[lax.rem(x + d, NX)], buf.at[x], ssem.at[0], rsem.at[0], x_peer(d), val)
            for d in range(1, NX)
        ]
        return x_batch(copies, buf, ssem, rsem)

    def matrix_total(copies, send, buf, tot):
        copies.wait_recv()
        total = buf[0].astype(F32)
        for i in range(1, NX):
            total = total + buf[i].astype(F32)
        tot[...] = total.astype(BF16)

    def matrix_end(buf, copies, zbuf, acc, out, forward):
        acc[...] = jnp.zeros(acc.shape, F32)
        add_arrivals(copies, zbuf, acc)
        running = acc[...]
        order = range(NX) if forward else range(NX - 1, -1, -1)
        for i in order:
            out[i] = running.astype(BF16)
            running = running + buf[i].astype(F32)

    def matrix_out(out, pre, ssem, rsem):
        pre[x] = out[x]
        copies = [
            bare(out.at[lax.rem(x + d, NX)], pre.at[x], ssem.at[0], rsem.at[0], x_peer(d), val)
            for d in range(1, NX)
        ]
        return x_batch(copies, pre, ssem, rsem)

    def scores_values(h):
        for b in range(blocks):
            for half in range(2):
                lo = 0 if half else CH
                own = slice(W + b * W, W + b * W + (half + 1) * CH)
                cols = slice(b * W + half * CH, b * W + (half + 1) * CH)
                num[h, :, cols] = nn(vx[h, :, own], ts[h, b, half, lo:])
                kc[h, :, cols] = nn(kx[h, :, own], cs[h, b, half, lo:])

    def windows(h, b):
        for half in range(2):
            t0 = b * W + half * CH
            win[h, :, t0 : t0 + CH] = nn(vx[h, :, t0 : t0 + 3 * CH], es[h, b, half])

    def scale_grads(h):
        for b in range(blocks):
            cols = slice(b * W, (b + 1) * W)
            wide = gx[h, :, cols].astype(F32)
            dn[h, :, cols] = (wide * rden[h, b, :1]).astype(BF16)

    def halo_values(h):
        for i in range(2):
            total = nt(gx[h, :, :CH], es[h, 0, 0, i * CH : (i + 1) * CH])
            if i == 1:
                total = total + nt(gx[h, :, CH:W], es[h, 0, 1, :CH])
            hv_send[h, :, i * CH : (i + 1) * CH] = total.astype(BF16)

    def turn_values(h, lo):
        for i in range(lo // CH, (vx.shape[2] if lo else W) // CH):
            vt[h, i * CH : (i + 1) * CH] = jnp.transpose(vx[h, :, i * CH : (i + 1) * CH].astype(F32)).astype(BF16)

    def deltas(h):
        for b in range(blocks):
            cols = slice(b * W, (b + 1) * W)
            dl[h, b, :1] = jnp.sum(gx[h, :, cols].astype(F32) * win[h, :, cols], axis=0, keepdims=True)

    def whole(pre, h):
        return jnp.concatenate([pre[i, h].astype(F32) for i in range(NX)], axis=0)

    def fold(grad, rows):
        xs = rows.astype(F32) * 0.5
        acc = 2.0 * (grad[:16] * xs + grad[128:144] * turn_up(xs, 8))
        for d in range(1, 8):
            one = grad[16 * d : 16 * d + 16]
            acc = acc + one * turn_up(xs, d) + turn_down(one * xs, d)
        return 0.5 * grad[LIN : LIN + 16] + (0.5 * ROOT_HALF) * acc

    def forward_state(h, b):
        state = whole(s_pre, h)
        for i in range(b):
            state = state + s_blk[h, i]
        return (state * weights).astype(BF16)

    def scatter(src, dst, ssem, rsem, b):
        copies = []
        span = pl.ds(b * W, W)
        for d in range(1, n_val):
            peer = val_peer(d)
            rows = pl.ds(pl.multiple_of(peer * part, part), part)
            copies.append(bare(src.at[:, rows, span], dst.at[my_heads, :, span], ssem.at[b], rsem.at[b], seq, peer))
        copies.append(pltpu.make_async_copy(src.at[:, mine, span], dst.at[my_heads, :, span], rsem.at[b]))
        sent = src.at[:, pl.ds(0, part * (n_val - 1)), span]
        return Batch(started, copies, dst.at[:, :, span], sent, ssem.at[b], rsem.at[b])

    def query_end(h):
        for b in range(blocks):
            cols = slice(b * W, (b + 1) * W)
            d_row = dd[h, b, :1]
            grad = nn(forward_state(h, b), dn[h, :, cols])
            grad = grad + jnp.concatenate([ncol[h, b]] * (W // 128), axis=1) * d_row
            local = dqa[h, :, cols] + d_row * kc[h, :, cols]
            dq_out[h, :, cols] = 0.25 * local + fold(grad, q_ref[h, :, cols])
            qd = (q_ref[h, :, cols].astype(F32) * d_row).astype(BF16)
            for half in range(2):
                lo = 0 if half else CH
                own = slice(W + b * W, W + b * W + (half + 1) * CH)
                dka[h, :, own] += nt(qd[:, half * CH : (half + 1) * CH], cs[h, b, half, lo:])

    def suffix_of(h, b):
        state = whole(u_pre, h)
        for i in range(b + 1, blocks):
            state = state + u_blk[h, i]
        return (state * weights).astype(BF16)

    def value_end(h, b):
        cols = slice(b * W, (b + 1) * W)
        inter = tn(suffix_of(h, b), fk[h, :, cols])
        dvb[h, :, cols] = (dva[h, :, cols] + inter).astype(BF16)

    def norm_rows():
        for h in range(heads):
            total = jnp.zeros((1, FR), F32)
            for b in range(blocks):
                row = nt(ones, fk[h, :, b * W : (b + 1) * W])[:1]
                nrow[h, b, :1] = row
                total = total + row
            nsend[h : h + 1, :] = total
        nsend[heads:, :] = jnp.zeros((8 - heads, FR), F32)

    def denominators():
        for h in range(heads):
            row = npre[h : h + 1, :]
            for b in range(blocks):
                column = as_column(row) * weights
                ncol[h, b] = column
                for i in range(W // 128):
                    lanes = slice(b * W + i * 128, b * W + (i + 1) * 128)
                    inter = jnp.sum(fq[h, :, lanes].astype(F32) * column, axis=0, keepdims=True)
                    here = slice(i * 128, (i + 1) * 128)
                    rden[h, b, :1, here] = 1.0 / (deni[h, b, :1, here] + inter)
                row = row + nrow[h, b, :1]

    def state_terms(feats, rows, off, blk, send):
        for h in range(heads):
            total = None
            for b in range(blocks):
                term = nt(feats[h, :, b * W : (b + 1) * W], rows[h, :, off + b * W : off + (b + 1) * W])
                blk[h, b] = term
                total = term if total is None else total + term
            matrix_send(h, total, send)

    def value_local(h, b):
        base = b * W
        total = nt(gx[h, :, base : base + CH], es[h, b, 0, 2 * CH :])
        total = total + nt(gx[h, :, base + CH : base + W], es[h, b, 1, CH : 2 * CH])
        total = total + nt(dn[h, :, base : base + CH], ts[h, b, 0, CH:])
        total = total + nt(dn[h, :, base + CH : base + W], ts[h, b, 1, :CH])
        last_half = nt(gx[h, :, base + CH : base + W], es[h, b, 1, 2 * CH :])
        last_half = last_half + nt(dn[h, :, base + CH : base + W], ts[h, b, 1, CH:])
        if b + 1 < blocks:
            after_base = base + W
            total = total + nt(gx[h, :, after_base : after_base + CH], es[h, b + 1, 0, :CH])
            last_half = last_half + nt(gx[h, :, after_base : after_base + CH], es[h, b + 1, 0, CH : 2 * CH])
            last_half = last_half + nt(gx[h, :, after_base + CH : after_base + W], es[h, b + 1, 1, :CH])
        dva[h, :, base : base + CH] = total
        dva[h, :, base + CH : base + W] = last_half

    def score_grads(h, b):
        for half in range(2):
            lo = 0 if half else CH
            t0 = b * W + half * CH
            cols = slice(t0, t0 + CH)
            keys = slice(t0, t0 + 3 * CH)
            own = slice(W + b * W, W + b * W + (half + 1) * CH)
            count = (half + 1) * CH
            mixing = nn(vt[h, keys], gx[h, :, cols])
            mixing_dn = nn(vt[h, own], dn[h, :, cols])
            gs = es[h, b, half].astype(F32) * (mixing - dl[h, b, :1, half * CH : (half + 1) * CH])
            taylor = cs[h, b, half, lo:].astype(F32) * mixing_dn
            gs = jnp.concatenate([gs[: 3 * CH - count], gs[3 * CH - count :] + taylor], axis=0).astype(BF16)
            dqa[h, :, cols] = nn(kx[h, :, keys], gs)
            dka[h, :, keys] += nt(q_ref[h, :, cols], gs)

    def linear_out(h):
        for b in range(blocks):
            cols = slice(b * W, (b + 1) * W)
            lin = (num[h, :, cols] + tn(forward_state(h, b), fq[h, :, cols])) * rden[h, b, :1]
            num[h, :, cols] = lin
            mix[h, :, cols] = (lin + win[h, :, cols]).astype(BF16)

    def den_grads(h):
        for b in range(blocks):
            cols = slice(b * W, (b + 1) * W)
            d_row = -jnp.sum(gx[h, :, cols].astype(F32) * num[h, :, cols], axis=0, keepdims=True) * rden[h, b, :1]
            dd[h, b, :1] = d_row
            drow[h, b, :1] = jnp.sum(nt(split_rows(d_row), fq[h, :, cols]), axis=0, keepdims=True)

    def den_rows():
        for h in range(heads):
            total = drow[h, 0, :1]
            for b in range(1, blocks):
                total = total + drow[h, b, :1]
            dsend[h : h + 1, :] = total
        dsend[heads:, :] = jnp.zeros((8 - heads, FR), F32)

    def key_end(h):
        row = dsuf[h : h + 1, :]
        for b in range(blocks - 1, -1, -1):
            cols = slice(b * W, (b + 1) * W)
            own = slice(W + b * W, W + (b + 1) * W)
            column = as_column(row) * weights
            grad = nn(suffix_of(h, b), vx[h, :, own])
            grad = grad + jnp.concatenate([column] * (W // 128), axis=1)
            dk_out[h, :, cols] = 0.25 * dka[h, :, own] + fold(grad, kx[h, :, own])
            row = row + drow[h, b, :1]

    build_features(kx, W, fk)
    norm_rows()
    n_1 = vector_x(nsend, nxbuf, nxs, nxr)
    n_1.start()
    build_features(q_ref, 0, fq)
    for b in range(1, blocks):
        each_head(functools.partial(lambda h, b: scores(h, b), b=b))
    vector_total(n_1, nxbuf, ntot)
    n_2 = along_z(ntot, nzbuf, nzs, nzr, True)
    key_halo.wait_recv()
    each_head(lambda h: scores(h, 0))
    v_copies[blocks - 1].wait_recv()
    value_halo.start()
    g_copies[0].start()
    vector_end(nxbuf, n_2, nzbuf, npre, True)
    denominators()
    for b in range(blocks - 1):
        v_copies[b].wait_recv()
    for b in range(1, blocks):
        g_copies[b].start()

    state_terms(fk, vx, W, s_blk, s_send)
    s_x[x] = s_send[x]
    s_1 = matrix_x(s_send, s_x, sxs, sxr)
    s_1.start()
    each_head(scores_values)
    for b in range(1, blocks):
        each_head(functools.partial(lambda h, b: windows(h, b), b=b))
    each_head(functools.partial(turn_values, lo=W))
    matrix_total(s_1, s_send, s_x, s_tot)
    s_2 = along_z(s_tot, s_z, szs, szr, True)
    value_halo.wait_recv()
    each_head(lambda h: windows(h, 0))

    g_copies[0].wait_recv()
    for b in range(1, blocks):
        g_copies[b].wait_recv()
    each_head(scale_grads)
    state_terms(fq, dn, 0, u_blk, u_send)
    u_x[x] = u_send[x]
    u_1 = matrix_x(u_send, u_x, uxs, uxr)
    u_1.start()
    each_head(halo_values)
    value_back.start()
    matrix_end(s_x, s_2, s_z, s_acc, s_out, True)
    s_3 = matrix_out(s_out, s_pre, sos, sor)
    s_3.start()
    each_head(lambda h: value_local(h, 0))
    matrix_total(u_1, u_send, u_x, u_tot)
    u_2 = along_z(u_tot, u_z, uzs, uzr, False)
    s_3.wait_recv()
    each_head(linear_out)
    for b in range(blocks):
        scatter(mix, mixed_out, mo_s, mo_r, b).start()
    for b in range(1, blocks):
        each_head(functools.partial(lambda h, b: value_local(h, b), b=b))
    each_head(den_grads)
    den_rows()
    d_1 = vector_x(dsend, dxbuf, dxs, dxr)
    d_1.start()
    each_head(functools.partial(turn_values, lo=0))
    each_head(deltas)
    dka[...] = jnp.zeros(dka.shape, F32)
    matrix_end(u_x, u_2, u_z, u_acc, u_out, False)
    u_3 = matrix_out(u_out, u_pre, uos, uor)
    u_3.start()
    each_head(lambda h: score_grads(h, 0))
    hk_send[...] = (0.25 * dka[:, :, :W]).astype(BF16)
    key_back.start()
    u_3.wait_recv()
    for b in range(blocks):
        if b == blocks - 1:
            value_back.wait_recv()

            @pl.when(outer)
            def _():
                dva[:, :, tokens - W :] += hv_recv[...].astype(F32)

        each_head(functools.partial(lambda h, b: value_end(h, b), b=b))
        scatter(dvb, dv_out, do_s, do_r, b).start()
    vector_total(d_1, dxbuf, dtot)
    d_2 = along_z(dtot, dzbuf, dzs, dzr, False)

    for b in range(1, blocks):
        each_head(functools.partial(lambda h, b: score_grads(h, b), b=b))
    each_head(query_end)
    key_back.wait_recv()

    @pl.when(outer)
    def _():
        dka[:, :, tokens:] += 4.0 * hk_recv[...].astype(F32)

    vector_end(dxbuf, d_2, dzbuf, dsuf, False)
    for h in range(heads):
        key_end(h)
    drain()


def hand_on(*refs):
    count = len(refs) // 3
    take_in, give_out = refs[-1].at[0], refs[-1].at[1]
    loads, stores = [], []
    for i in range(count):
        source, target, held = refs[i], refs[count + i], refs[2 * count + i]
        loads.append(pltpu.make_async_copy(source, held, take_in.at[i]))
        stores.append(pltpu.make_async_copy(held, target, give_out.at[i]))
    for c in loads:
        c.start()
    for load, store in zip(loads, stores):
        load.wait()
        store.start()
    for c in stores:
        c.wait()


def local(queries, keys, values, out_grad):
    heads, width, tokens = queries.shape
    all_heads, part, _ = values.shape
    n_seq, n_val = lax.axis_size("seq"), lax.axis_size("val")
    nz = n_seq // NX
    blocks = tokens // W
    ev = part * n_val
    vm = pltpu.VMEM
    dma = pltpu.SemaphoreType.DMA
    row = (heads, blocks, 8, W)

    def matrix_scratch():
        return [
            vm((heads, blocks, FR, ev), F32),
            vm((NX, heads, QR, ev), BF16),
            vm((NX, heads, QR, ev), BF16),
            vm((heads, QR, ev), BF16),
            vm((nz, heads, QR, ev), BF16),
            vm((heads, QR, ev), F32),
            vm((NX, heads, QR, ev), BF16),
            vm((NX, heads, QR, ev), BF16),
        ]

    def vector_scratch():
        return [
            vm((8, FR), F32),
            vm((NX, 8, FR), F32),
            vm((8, FR), F32),
            vm((nz, 8, FR), F32),
            vm((8, FR), F32),
        ]

    scratch = [
        vm(queries.shape, BF16),
        vm((heads, width, W + tokens), BF16),
        vm((heads, ev, W + tokens), BF16),
        vm((heads, W + tokens, ev), BF16),
        vm((heads, ev, tokens), BF16),
        vm((heads, FR, tokens), BF16),
        vm((heads, FR, tokens), BF16),
        vm((heads, blocks, 2, 3 * CH, CH), BF16),
        vm((heads, blocks, 2, 2 * CH, CH), BF16),
        vm((heads, blocks, 2, 2 * CH, CH), BF16),
        vm((heads, ev, tokens), F32),
        vm((heads, ev, tokens), F32),
        vm((heads, width, tokens), F32),
        vm(row, F32),
        vm(row, F32),
        vm(row, F32),
        vm(row, F32),
        vm((heads, ev, tokens), BF16),
        vm((heads, width, tokens), F32),
        vm((heads, width, W + tokens), F32),
        vm((heads, ev, tokens), F32),
        vm((heads, ev, tokens), BF16),
        vm((heads, ev, tokens), BF16),
        vm((heads, blocks, 8, FR), F32),
        *vector_scratch(),
        vm((heads, blocks, FR, 128), F32),
        vm((heads, blocks, 8, FR), F32),
        *vector_scratch(),
        *matrix_scratch(),
        *matrix_scratch(),
        vm((heads, width, W), BF16),
        vm((heads, ev, W), BF16),
        vm((heads, width, W), BF16),
        vm((heads, ev, W), BF16),
        *[dma((blocks,)) for _ in range(8)],
        *[dma((2,)) for _ in range(5)],
        *[dma((1,)), dma((1,)), dma((nz - 1,)), dma((nz - 1,))] * 2,
        *[dma((1,)), dma((1,)), dma((nz - 1,)), dma((nz - 1,)), dma((1,)), dma((1,))] * 2,
    ]
    vmem = pl.BlockSpec(memory_space=pltpu.VMEM)
    hbm = pl.BlockSpec(memory_space=pl.ANY)
    outs = pl.pallas_call(
        functools.partial(kernel, n_seq, n_val),
        out_shape=(
            jax.ShapeDtypeStruct(values.shape, BF16),
            jax.ShapeDtypeStruct(queries.shape, F32),
            jax.ShapeDtypeStruct(keys.shape, F32),
            jax.ShapeDtypeStruct(values.shape, BF16),
        ),
        in_specs=[hbm, hbm, hbm, hbm],
        out_specs=(hbm, vmem, vmem, hbm),
        scratch_shapes=scratch,
        compiler_params=pltpu.CompilerParams(
            collective_id=0, has_side_effects=True, vmem_limit_bytes=56 << 20
        ),
        name="based_layer",
    )(queries, keys, values, out_grad)
    return pl.pallas_call(
        hand_on,
        out_shape=tuple(jax.ShapeDtypeStruct(o.shape, o.dtype) for o in outs),
        in_specs=[hbm] * len(outs),
        out_specs=(hbm,) * len(outs),
        scratch_shapes=[*[vm(o.shape, o.dtype) for o in outs], dma((2, len(outs)))],
        name="hand_on",
    )(*outs)


def solution(mesh):
    in_specs = (
        P("val", None, "seq"),
        P("val", None, "seq"),
        P(None, "val", "seq"),
        P(None, "val", "seq"),
    )
    out_specs = (
        P(None, "val", "seq"),
        P("val", None, "seq"),
        P("val", None, "seq"),
        P(None, "val", "seq"),
    )
    return jax.shard_map(local, mesh=mesh, in_specs=in_specs, out_specs=out_specs, check_vma=False)
```

```python
import functools

import jax
import jax.numpy as jnp
from jax import lax
from jax.experimental import pallas as pl
from jax.experimental.pallas import tpu as pltpu
from jax.sharding import PartitionSpec as P

W = 512
CH = 256
NX = 4
FR = 192
QR = FR // NX
LIN = 144
ROOT_HALF = 0.7071067811865476
NEG_LARGE = -1e30
MESH = pl.DeviceIdType.MESH
F32 = jnp.float32
BF16 = jnp.bfloat16


def dot(a, b, ca, cb):
    return lax.dot_general(a, b, (((ca,), (cb,)), ((), ())), preferred_element_type=F32)


def nn(a, b):
    return dot(a, b, 1, 0)


def nt(a, b):
    return dot(a, b, 1, 1)


def tn(a, b):
    return dot(a, b, 0, 0)


def turn_up(x, d):
    return jnp.concatenate([x[d:], x[:d]], axis=0) if d else x


def turn_down(x, d):
    return turn_up(x, 16 - d)


def split_rows(row):
    high = row.astype(BF16).astype(F32)
    low = row - high
    index = lax.broadcasted_iota(jnp.int32, (16, row.shape[1]), 0)
    return jnp.where(index == 0, high, jnp.where(index == 1, low, 0.0)).astype(BF16)


def when(condition, action):
    if condition is None:
        action()
    else:
        pl.when(condition)(action)


class Copy:
    def __init__(self, started, make, sends=None, takes=None):
        self.started, self.make, self.sends, self.takes = started, make, sends, takes
        self.waits = {"send", "recv"}

    def start(self):
        when(self.sends, lambda: self.make().start())
        self.started.append(self)

    def wait_recv(self):
        self.waits.discard("recv")
        when(self.takes, lambda: self.make().wait_recv())

    def finish(self):
        if "recv" in self.waits:
            self.wait_recv()
        when(self.sends, lambda: self.make().wait_send())


class Batch:
    def __init__(self, started, copies, whole, sent, ssem, rsem):
        self.started, self.copies, self.whole, self.sent, self.ssem, self.rsem = started, copies, whole, sent, ssem, rsem
        self.waiting = True

    def start(self):
        for c in self.copies:
            c.start()
        self.started.append(self)

    def wait_recv(self):
        self.waiting = False
        pltpu.make_async_copy(self.whole, self.whole, self.rsem).wait()

    def finish(self):
        if self.waiting:
            self.wait_recv()
        pltpu.make_async_copy(self.sent, self.sent, self.ssem).wait()


def stack_rows(rows):
    index = lax.broadcasted_iota(jnp.int32, (8, rows[0].shape[1]), 0)
    out = jnp.zeros((8, rows[0].shape[1]), F32)
    for i, row in enumerate(rows):
        out = jnp.where(index == i, row, out)
    return out


def pair_weights(columns):
    row = lax.broadcasted_iota(jnp.int32, (FR, columns), 0)
    return jnp.where(jnp.logical_and(row >= 16, row < 128), 2.0, 1.0)


def kernel(
    n_seq,
    n_val,
    q_hbm,
    k_hbm,
    v_hbm,
    g_hbm,
    mixed_out,
    dq_out,
    dk_out,
    dv_out,
    q_ref,
    kx,
    vx,
    vt,
    gx,
    fq,
    fk,
    es,
    cs,
    ts,
    num,
    win,
    kc,
    deni,
    rden,
    dd,
    dl,
    dn,
    dqa,
    dka,
    dva,
    mix,
    dvb,
    nrow,
    nsend,
    nxbuf,
    ntot,
    nzbuf,
    npre,
    ncol,
    drow,
    dsend,
    dxbuf,
    dtot,
    dzbuf,
    dsuf,
    s_blk,
    s_send,
    s_x,
    s_tot,
    s_z,
    s_acc,
    s_out,
    s_pre,
    u_blk,
    u_send,
    u_x,
    u_tot,
    u_z,
    u_acc,
    u_out,
    u_pre,
    hk_send,
    hv_send,
    hk_recv,
    hv_recv,
    va_s,
    va_r,
    ga_s,
    ga_r,
    mo_s,
    mo_r,
    do_s,
    do_r,
    loc,
    kh,
    vh,
    gkh,
    gvh,
    nxs,
    nxr,
    nzs,
    nzr,
    dxs,
    dxr,
    dzs,
    dzr,
    sxs,
    sxr,
    szs,
    szr,
    sos,
    sor,
    uxs,
    uxr,
    uzs,
    uzr,
    uos,
    uor,
):
    heads = q_ref.shape[0]
    tokens = q_ref.shape[2]
    blocks = tokens // W
    part = v_hbm.shape[1]
    nz = n_seq // NX
    seq = lax.axis_index("seq")
    val = lax.axis_index("val")
    z = seq // NX
    x = lax.rem(seq, NX)
    first = seq == 0
    last = seq == n_seq - 1
    after = lax.rem(seq + 1, n_seq)
    ahead = lax.rem(seq + n_seq - 1, n_seq)

    started = []

    def bare(src, dst, ssem, rsem, s, v):
        return pltpu.make_async_remote_copy(
            src_ref=src, dst_ref=dst, send_sem=ssem, recv_sem=rsem, device_id=(s, v), device_id_type=MESH
        )

    def remote(src, dst, ssem, rsem, s, v, sends=None, takes=None):
        return Copy(started, lambda: bare(src, dst, ssem, rsem, s, v), sends, takes)

    def drain():
        for c in started:
            c.finish()

    def val_peer(d):
        return lax.rem(val + d, n_val)

    def x_peer(d):
        return z * NX + lax.rem(x + d, NX)

    k_load = pltpu.make_async_copy(k_hbm, kx.at[:, :, pl.ds(W, tokens)], loc.at[0])
    q_load = pltpu.make_async_copy(q_hbm, q_ref, loc.at[1])
    k_load.start()
    q_load.start()
    barrier = pltpu.get_barrier_semaphore()

    def greet(s, v):
        pl.semaphore_signal(barrier, inc=1, device_id=(s, v), device_id_type=MESH)

    for d in range(1, n_val):
        greet(seq, val_peer(d))
    for d in range(1, NX):
        greet(x_peer(d), val)
    for d in range(1, nz):
        greet(lax.rem(z + d, nz) * NX + x, val)
    greet(after, val)
    greet(ahead, val)

    @pl.when(first)
    def _():
        kx[:, :, :W] = jnp.zeros((heads, 16, W), BF16)
        vx[:, :, :W] = jnp.zeros((heads, 128, W), BF16)

    pl.semaphore_wait(barrier, (n_val - 1) + (NX - 1) + (nz - 1) + 2)

    mine = pl.ds(pl.multiple_of(val * part, part), part)
    my_heads = pl.ds(val * heads, heads)

    def gather_copies(src, dst, off, ssem, rsem, b):
        copies = []
        span, to = pl.ds(b * W, W), pl.ds(off + b * W, W)
        for d in range(1, n_val):
            peer = val_peer(d)
            theirs = pl.ds(peer * heads, heads)
            copies.append(bare(src.at[theirs, :, span], dst.at[:, mine, to], ssem.at[b], rsem.at[b], seq, peer))
        copies.append(pltpu.make_async_copy(src.at[my_heads, :, span], dst.at[:, mine, to], rsem.at[b]))
        sent = dst.at[:, pl.ds(0, part * (n_val - 1)), to]
        return Batch(started, copies, dst.at[:, :, to], sent, ssem.at[b], rsem.at[b])

    v_copies = [gather_copies(v_hbm, vx, W, va_s, va_r, b) for b in range(blocks)]
    g_copies = [gather_copies(g_hbm, gx, 0, ga_s, ga_r, b) for b in range(blocks)]
    inner, outer = jnp.logical_not(first), jnp.logical_not(last)
    key_halo = remote(
        kx.at[:, :, pl.ds(tokens, W)], kx.at[:, :, pl.ds(0, W)], kh.at[0], kh.at[1], after, val, outer, inner
    )
    value_halo = remote(
        vx.at[:, :, pl.ds(tokens, W)], vx.at[:, :, pl.ds(0, W)], vh.at[0], vh.at[1], after, val, outer, inner
    )
    key_back = remote(hk_send, hk_recv, gkh.at[0], gkh.at[1], ahead, val, inner, outer)
    value_back = remote(hv_send, hv_recv, gvh.at[0], gvh.at[1], ahead, val, inner, outer)
    v_copies[blocks - 1].start()
    for b in range(blocks - 1):
        v_copies[b].start()
    k_load.wait()
    q_load.wait()
    key_halo.start()

    const = jnp.where(lax.broadcasted_iota(jnp.int32, (FR - LIN - 16, tokens), 0) == 0, 1.0, 0.0).astype(BF16)
    row_id = lax.broadcasted_iota(jnp.int32, (CH, CH), 0)
    col_id = lax.broadcasted_iota(jnp.int32, (CH, CH), 1)
    weights = pair_weights(128)
    ones = jnp.ones((16, W), BF16)

    def build_features(src, off, dst):
        def one(h, carry):
            xs = src[h, :, off : off + tokens].astype(F32) * 0.5
            for d in range(9):
                dst[h, 16 * d : 16 * d + 16, :] = (xs * turn_up(xs, d) * ROOT_HALF).astype(BF16)
            dst[h, LIN : LIN + 16, :] = xs.astype(BF16)
            dst[h, LIN + 16 :, :] = const
            return carry

        lax.fori_loop(0, heads, one, 0)

    def x_batch(copies, buf, ssem, rsem):
        bulk = buf.at[pl.ds(0, NX - 1)]
        return Batch(started, copies, bulk, bulk, ssem.at[0], rsem.at[0])

    def vector_x(send, buf, ssem, rsem):
        buf[x] = send[...]
        copies = [bare(send, buf.at[x], ssem.at[0], rsem.at[0], x_peer(d), val) for d in range(1, NX)]
        return x_batch(copies, buf, ssem, rsem)

    def scores(h, b):
        mask = row_id <= col_id
        for half in range(2):
            t0 = b * W + half * CH
            qs = (q_ref[h, :, t0 : t0 + CH].astype(F32) * 0.25).astype(BF16)
            s = tn(kx[h, :, t0 : t0 + 3 * CH], qs)
            s_old, s_mid, s_own = s[:CH], s[CH : 2 * CH], s[2 * CH :]
            w_mid = s_mid
            if b == 0:
                gone = jnp.where(first, NEG_LARGE, 0.0)
                s_old = s_old + gone
                if half == 0:
                    w_mid = s_mid + gone
            s_diag = jnp.where(mask, s_own, s_old)
            top = jnp.maximum(
                jnp.max(s_diag, axis=0, keepdims=True), jnp.max(w_mid, axis=0, keepdims=True)
            )
            e_diag = jnp.exp(s_diag - top)
            e_mid = jnp.exp(w_mid - top)
            sums = jnp.sum(e_diag, axis=0, keepdims=True) + jnp.sum(e_mid, axis=0, keepdims=True)
            scale = 1.0 / sums
            p_diag = e_diag * scale
            es[h, b, half, :CH] = jnp.where(mask, 0.0, p_diag).astype(BF16)
            es[h, b, half, CH : 2 * CH] = (e_mid * scale).astype(BF16)
            es[h, b, half, 2 * CH :] = jnp.where(mask, p_diag, 0.0).astype(BF16)
            c_own = 1.0 + s_own
            t_own = jnp.where(mask, 0.5 * (c_own * c_own) + 0.5, 0.0)
            den = jnp.sum(t_own, axis=0, keepdims=True)
            cs[h, b, half, CH:] = jnp.where(mask, c_own, 0.0).astype(BF16)
            ts[h, b, half, CH:] = t_own.astype(BF16)
            if half == 1:
                c_mid = 1.0 + s_mid
                t_mid = 0.5 * (c_mid * c_mid) + 0.5
                den = den + jnp.sum(t_mid, axis=0, keepdims=True)
                cs[h, b, half, :CH] = c_mid.astype(BF16)
                ts[h, b, half, :CH] = t_mid.astype(BF16)
            deni[h, b, :1, half * CH : (half + 1) * CH] = den

    def each_head(body):
        def one(h, carry):
            body(h)
            return carry

        lax.fori_loop(0, heads, one, 0)

    def along_z(tot, buf, ssem, rsem, forward):
        copies = []
        for d in range(1, nz):
            to = z + d if forward else z - d
            up, down = z + d < nz, z >= d
            sends, takes = (up, down) if forward else (down, up)
            copies.append(remote(tot, buf.at[d], ssem.at[d - 1], rsem.at[d - 1], to * NX + x, val, sends, takes))
            copies[-1].start()
        return copies

    def vector_total(copies, buf, tot):
        copies.wait_recv()
        total = buf[0]
        for i in range(1, NX):
            total = total + buf[i]
        tot[...] = total

    def vector_end(xbuf, copies, zbuf, out, forward):
        acc = jnp.zeros((8, FR), F32)
        for i in range(NX):
            taken = (i < x) if forward else (i > x)
            acc = acc + jnp.where(taken, xbuf[i], 0.0)
        out[...] = acc
        add_arrivals(copies, zbuf, out)

    def add_arrivals(copies, zbuf, out):
        for i, c in enumerate(copies):
            c.wait_recv()

            def add():
                out[...] += zbuf[i + 1].astype(F32)

            when(c.takes, add)

    def as_column(row):
        return jnp.transpose(jnp.broadcast_to(row, (128, row.shape[1])))

    def matrix_send(h, total, send):
        low = total.astype(BF16)
        for i in range(NX):
            send[i, h] = low[i * QR : (i + 1) * QR]

    def matrix_x(send, buf, ssem, rsem):
        copies = [
            bare(send.at[lax.rem(x + d, NX)], buf.at[x], ssem.at[0], rsem.at[0], x_peer(d), val)
            for d in range(1, NX)
        ]
        return x_batch(copies, buf, ssem, rsem)

    def matrix_total(copies, send, buf, tot):
        copies.wait_recv()
        total = buf[0].astype(F32)
        for i in range(1, NX):
            total = total + buf[i].astype(F32)
        tot[...] = total.astype(BF16)

    def matrix_end(buf, copies, zbuf, acc, out, forward):
        acc[...] = jnp.zeros(acc.shape, F32)
        add_arrivals(copies, zbuf, acc)
        running = acc[...]
        order = range(NX) if forward else range(NX - 1, -1, -1)
        for i in order:
            out[i] = running.astype(BF16)
            running = running + buf[i].astype(F32)

    def matrix_out(out, pre, ssem, rsem):
        pre[x] = out[x]
        copies = [
            bare(out.at[lax.rem(x + d, NX)], pre.at[x], ssem.at[0], rsem.at[0], x_peer(d), val)
            for d in range(1, NX)
        ]
        return x_batch(copies, pre, ssem, rsem)

    def scores_values(h):
        for b in range(blocks):
            for half in range(2):
                lo = 0 if half else CH
                own = slice(W + b * W, W + b * W + (half + 1) * CH)
                cols = slice(b * W + half * CH, b * W + (half + 1) * CH)
                num[h, :, cols] = nn(vx[h, :, own], ts[h, b, half, lo:])
                kc[h, :, cols] = nn(kx[h, :, own], cs[h, b, half, lo:])

    def windows(h, b):
        for half in range(2):
            t0 = b * W + half * CH
            win[h, :, t0 : t0 + CH] = nn(vx[h, :, t0 : t0 + 3 * CH], es[h, b, half])

    def scale_grads(h):
        for b in range(blocks):
            cols = slice(b * W, (b + 1) * W)
            wide = gx[h, :, cols].astype(F32)
            dn[h, :, cols] = (wide * rden[h, b, :1]).astype(BF16)

    def halo_values(h):
        for i in range(2):
            total = nt(gx[h, :, :CH], es[h, 0, 0, i * CH : (i + 1) * CH])
            if i == 1:
                total = total + nt(gx[h, :, CH:W], es[h, 0, 1, :CH])
            hv_send[h, :, i * CH : (i + 1) * CH] = total.astype(BF16)

    def turn_values(h, lo):
        for i in range(lo // CH, (vx.shape[2] if lo else W) // CH):
            vt[h, i * CH : (i + 1) * CH] = jnp.transpose(vx[h, :, i * CH : (i + 1) * CH].astype(F32)).astype(BF16)

    def deltas(h):
        for b in range(blocks):
            cols = slice(b * W, (b + 1) * W)
            dl[h, b, :1] = jnp.sum(gx[h, :, cols].astype(F32) * win[h, :, cols], axis=0, keepdims=True)

    def whole(pre, h):
        return jnp.concatenate([pre[i, h].astype(F32) for i in range(NX)], axis=0)

    def fold(grad, rows):
        xs = rows.astype(F32) * 0.5
        acc = 2.0 * (grad[:16] * xs + grad[128:144] * turn_up(xs, 8))
        for d in range(1, 8):
            one = grad[16 * d : 16 * d + 16]
            acc = acc + one * turn_up(xs, d) + turn_down(one * xs, d)
        return 0.5 * grad[LIN : LIN + 16] + (0.5 * ROOT_HALF) * acc

    def forward_state(h, b):
        state = whole(s_pre, h)
        for i in range(b):
            state = state + s_blk[h, i]
        return (state * weights).astype(BF16)

    def scatter(src, dst, ssem, rsem, b):
        copies = []
        span = pl.ds(b * W, W)
        for d in range(1, n_val):
            peer = val_peer(d)
            rows = pl.ds(pl.multiple_of(peer * part, part), part)
            copies.append(bare(src.at[:, rows, span], dst.at[my_heads, :, span], ssem.at[b], rsem.at[b], seq, peer))
        copies.append(pltpu.make_async_copy(src.at[:, mine, span], dst.at[my_heads, :, span], rsem.at[b]))
        sent = src.at[:, pl.ds(0, part * (n_val - 1)), span]
        return Batch(started, copies, dst.at[:, :, span], sent, ssem.at[b], rsem.at[b])

    def query_end(h):
        for b in range(blocks):
            cols = slice(b * W, (b + 1) * W)
            d_row = dd[h, b, :1]
            grad = nn(forward_state(h, b), dn[h, :, cols])
            grad = grad + jnp.concatenate([ncol[h, b]] * (W // 128), axis=1) * d_row
            local = dqa[h, :, cols] + d_row * kc[h, :, cols]
            dq_out[h, :, cols] = 0.25 * local + fold(grad, q_ref[h, :, cols])
            qd = (q_ref[h, :, cols].astype(F32) * d_row).astype(BF16)
            for half in range(2):
                lo = 0 if half else CH
                own = slice(W + b * W, W + b * W + (half + 1) * CH)
                dka[h, :, own] += nt(qd[:, half * CH : (half + 1) * CH], cs[h, b, half, lo:])

    def suffix_of(h, b):
        state = whole(u_pre, h)
        for i in range(b + 1, blocks):
            state = state + u_blk[h, i]
        return (state * weights).astype(BF16)

    def value_end(h, b):
        cols = slice(b * W, (b + 1) * W)
        inter = tn(suffix_of(h, b), fk[h, :, cols])
        dvb[h, :, cols] = (dva[h, :, cols] + inter).astype(BF16)

    def norm_rows():
        totals = []
        for h in range(heads):
            total = jnp.zeros((1, FR), F32)
            for b in range(blocks):
                row = nt(ones, fk[h, :, b * W : (b + 1) * W])[:1]
                nrow[h, b, :1] = row
                total = total + row
            totals.append(total)
        nsend[...] = stack_rows(totals)

    def denominators():
        for h in range(heads):
            row = npre[...][h : h + 1]
            for b in range(blocks):
                column = as_column(row) * weights
                ncol[h, b] = column
                for i in range(W // 128):
                    lanes = slice(b * W + i * 128, b * W + (i + 1) * 128)
                    inter = jnp.sum(fq[h, :, lanes].astype(F32) * column, axis=0, keepdims=True)
                    here = slice(i * 128, (i + 1) * 128)
                    rden[h, b, :1, here] = 1.0 / (deni[h, b, :1, here] + inter)
                row = row + nrow[h, b, :1]

    def state_terms(feats, rows, off, blk, send):
        for h in range(heads):
            total = None
            for b in range(blocks):
                term = nt(feats[h, :, b * W : (b + 1) * W], rows[h, :, off + b * W : off + (b + 1) * W])
                blk[h, b] = term
                total = term if total is None else total + term
            matrix_send(h, total, send)

    def value_local(h, b):
        base = b * W
        total = nt(gx[h, :, base : base + CH], es[h, b, 0, 2 * CH :])
        total = total + nt(gx[h, :, base + CH : base + W], es[h, b, 1, CH : 2 * CH])
        total = total + nt(dn[h, :, base : base + CH], ts[h, b, 0, CH:])
        total = total + nt(dn[h, :, base + CH : base + W], ts[h, b, 1, :CH])
        last_half = nt(gx[h, :, base + CH : base + W], es[h, b, 1, 2 * CH :])
        last_half = last_half + nt(dn[h, :, base + CH : base + W], ts[h, b, 1, CH:])
        if b + 1 < blocks:
            after_base = base + W
            total = total + nt(gx[h, :, after_base : after_base + CH], es[h, b + 1, 0, :CH])
            last_half = last_half + nt(gx[h, :, after_base : after_base + CH], es[h, b + 1, 0, CH : 2 * CH])
            last_half = last_half + nt(gx[h, :, after_base + CH : after_base + W], es[h, b + 1, 1, :CH])
        dva[h, :, base : base + CH] = total
        dva[h, :, base + CH : base + W] = last_half

    def score_grads(h, b):
        for half in range(2):
            lo = 0 if half else CH
            t0 = b * W + half * CH
            cols = slice(t0, t0 + CH)
            keys = slice(t0, t0 + 3 * CH)
            own = slice(W + b * W, W + b * W + (half + 1) * CH)
            count = (half + 1) * CH
            mixing = nn(vt[h, keys], gx[h, :, cols])
            mixing_dn = nn(vt[h, own], dn[h, :, cols])
            gs = es[h, b, half].astype(F32) * (mixing - dl[h, b, :1, half * CH : (half + 1) * CH])
            taylor = cs[h, b, half, lo:].astype(F32) * mixing_dn
            gs = jnp.concatenate([gs[: 3 * CH - count], gs[3 * CH - count :] + taylor], axis=0).astype(BF16)
            dqa[h, :, cols] = nn(kx[h, :, keys], gs)
            dka[h, :, keys] += nt(q_ref[h, :, cols], gs)

    def linear_out(h):
        for b in range(blocks):
            cols = slice(b * W, (b + 1) * W)
            lin = (num[h, :, cols] + tn(forward_state(h, b), fq[h, :, cols])) * rden[h, b, :1]
            num[h, :, cols] = lin
            mix[h, :, cols] = (lin + win[h, :, cols]).astype(BF16)

    def den_grads(h):
        for b in range(blocks):
            cols = slice(b * W, (b + 1) * W)
            d_row = -jnp.sum(gx[h, :, cols].astype(F32) * num[h, :, cols], axis=0, keepdims=True) * rden[h, b, :1]
            dd[h, b, :1] = d_row
            drow[h, b, :1] = jnp.sum(nt(split_rows(d_row), fq[h, :, cols]), axis=0, keepdims=True)

    def den_rows():
        totals = []
        for h in range(heads):
            total = drow[h, 0, :1]
            for b in range(1, blocks):
                total = total + drow[h, b, :1]
            totals.append(total)
        dsend[...] = stack_rows(totals)

    def key_end(h):
        row = dsuf[...][h : h + 1]
        for b in range(blocks - 1, -1, -1):
            cols = slice(b * W, (b + 1) * W)
            own = slice(W + b * W, W + (b + 1) * W)
            column = as_column(row) * weights
            grad = nn(suffix_of(h, b), vx[h, :, own])
            grad = grad + jnp.concatenate([column] * (W // 128), axis=1)
            dk_out[h, :, cols] = 0.25 * dka[h, :, own] + fold(grad, kx[h, :, own])
            row = row + drow[h, b, :1]

    build_features(kx, W, fk)
    norm_rows()
    n_1 = vector_x(nsend, nxbuf, nxs, nxr)
    n_1.start()
    build_features(q_ref, 0, fq)
    for b in range(1, blocks):
        each_head(functools.partial(lambda h, b: scores(h, b), b=b))
    vector_total(n_1, nxbuf, ntot)
    n_2 = along_z(ntot, nzbuf, nzs, nzr, True)
    key_halo.wait_recv()
    each_head(lambda h: scores(h, 0))
    v_copies[blocks - 1].wait_recv()
    value_halo.start()
    g_copies[0].start()
    vector_end(nxbuf, n_2, nzbuf, npre, True)
    denominators()
    for b in range(blocks - 1):
        v_copies[b].wait_recv()
    for b in range(1, blocks):
        g_copies[b].start()

    state_terms(fk, vx, W, s_blk, s_send)
    s_x[x] = s_send[x]
    s_1 = matrix_x(s_send, s_x, sxs, sxr)
    s_1.start()
    each_head(scores_values)
    for b in range(1, blocks):
        each_head(functools.partial(lambda h, b: windows(h, b), b=b))
    each_head(functools.partial(turn_values, lo=W))
    matrix_total(s_1, s_send, s_x, s_tot)
    s_2 = along_z(s_tot, s_z, szs, szr, True)
    value_halo.wait_recv()
    each_head(lambda h: windows(h, 0))

    g_copies[0].wait_recv()
    for b in range(1, blocks):
        g_copies[b].wait_recv()
    each_head(scale_grads)
    state_terms(fq, dn, 0, u_blk, u_send)
    u_x[x] = u_send[x]
    u_1 = matrix_x(u_send, u_x, uxs, uxr)
    u_1.start()
    each_head(halo_values)
    value_back.start()
    matrix_end(s_x, s_2, s_z, s_acc, s_out, True)
    s_3 = matrix_out(s_out, s_pre, sos, sor)
    s_3.start()
    each_head(lambda h: value_local(h, 0))
    matrix_total(u_1, u_send, u_x, u_tot)
    u_2 = along_z(u_tot, u_z, uzs, uzr, False)
    s_3.wait_recv()
    each_head(linear_out)
    for b in range(blocks):
        scatter(mix, mixed_out, mo_s, mo_r, b).start()
    for b in range(1, blocks):
        each_head(functools.partial(lambda h, b: value_local(h, b), b=b))
    each_head(den_grads)
    den_rows()
    d_1 = vector_x(dsend, dxbuf, dxs, dxr)
    d_1.start()
    each_head(functools.partial(turn_values, lo=0))
    each_head(deltas)
    dka[...] = jnp.zeros(dka.shape, F32)
    matrix_end(u_x, u_2, u_z, u_acc, u_out, False)
    u_3 = matrix_out(u_out, u_pre, uos, uor)
    u_3.start()
    each_head(lambda h: score_grads(h, 0))
    hk_send[...] = (0.25 * dka[:, :, :W]).astype(BF16)
    key_back.start()
    u_3.wait_recv()
    for b in range(blocks):
        if b == blocks - 1:
            value_back.wait_recv()

            @pl.when(outer)
            def _():
                dva[:, :, tokens - W :] += hv_recv[...].astype(F32)

        each_head(functools.partial(lambda h, b: value_end(h, b), b=b))
        scatter(dvb, dv_out, do_s, do_r, b).start()
    vector_total(d_1, dxbuf, dtot)
    d_2 = along_z(dtot, dzbuf, dzs, dzr, False)

    for b in range(1, blocks):
        each_head(functools.partial(lambda h, b: score_grads(h, b), b=b))
    each_head(query_end)
    key_back.wait_recv()

    @pl.when(outer)
    def _():
        dka[:, :, tokens:] += 4.0 * hk_recv[...].astype(F32)

    vector_end(dxbuf, d_2, dzbuf, dsuf, False)
    for h in range(heads):
        key_end(h)
    drain()


def hand_on(*refs):
    count = len(refs) // 3
    take_in, give_out = refs[-1].at[0], refs[-1].at[1]
    loads, stores = [], []
    for i in range(count):
        source, target, held = refs[i], refs[count + i], refs[2 * count + i]
        loads.append(pltpu.make_async_copy(source, held, take_in.at[i]))
        stores.append(pltpu.make_async_copy(held, target, give_out.at[i]))
    for c in loads:
        c.start()
    for load, store in zip(loads, stores):
        load.wait()
        store.start()
    for c in stores:
        c.wait()


def local(queries, keys, values, out_grad):
    heads, width, tokens = queries.shape
    all_heads, part, _ = values.shape
    n_seq, n_val = lax.axis_size("seq"), lax.axis_size("val")
    nz = n_seq // NX
    blocks = tokens // W
    ev = part * n_val
    vm = pltpu.VMEM
    dma = pltpu.SemaphoreType.DMA
    row = (heads, blocks, 8, W)

    def matrix_scratch():
        return [
            vm((heads, blocks, FR, ev), F32),
            vm((NX, heads, QR, ev), BF16),
            vm((NX, heads, QR, ev), BF16),
            vm((heads, QR, ev), BF16),
            vm((nz, heads, QR, ev), BF16),
            vm((heads, QR, ev), F32),
            vm((NX, heads, QR, ev), BF16),
            vm((NX, heads, QR, ev), BF16),
        ]

    def vector_scratch():
        return [
            vm((8, FR), F32),
            vm((NX, 8, FR), F32),
            vm((8, FR), F32),
            vm((nz, 8, FR), F32),
            vm((8, FR), F32),
        ]

    scratch = [
        vm(queries.shape, BF16),
        vm((heads, width, W + tokens), BF16),
        vm((heads, ev, W + tokens), BF16),
        vm((heads, W + tokens, ev), BF16),
        vm((heads, ev, tokens), BF16),
        vm((heads, FR, tokens), BF16),
        vm((heads, FR, tokens), BF16),
        vm((heads, blocks, 2, 3 * CH, CH), BF16),
        vm((heads, blocks, 2, 2 * CH, CH), BF16),
        vm((heads, blocks, 2, 2 * CH, CH), BF16),
        vm((heads, ev, tokens), F32),
        vm((heads, ev, tokens), F32),
        vm((heads, width, tokens), F32),
        vm(row, F32),
        vm(row, F32),
        vm(row, F32),
        vm(row, F32),
        vm((heads, ev, tokens), BF16),
        vm((heads, width, tokens), F32),
        vm((heads, width, W + tokens), F32),
        vm((heads, ev, tokens), F32),
        vm((heads, ev, tokens), BF16),
        vm((heads, ev, tokens), BF16),
        vm((heads, blocks, 8, FR), F32),
        *vector_scratch(),
        vm((heads, blocks, FR, 128), F32),
        vm((heads, blocks, 8, FR), F32),
        *vector_scratch(),
        *matrix_scratch(),
        *matrix_scratch(),
        vm((heads, width, W), BF16),
        vm((heads, ev, W), BF16),
        vm((heads, width, W), BF16),
        vm((heads, ev, W), BF16),
        *[dma((blocks,)) for _ in range(8)],
        *[dma((2,)) for _ in range(5)],
        *[dma((1,)), dma((1,)), dma((nz - 1,)), dma((nz - 1,))] * 2,
        *[dma((1,)), dma((1,)), dma((nz - 1,)), dma((nz - 1,)), dma((1,)), dma((1,))] * 2,
    ]
    vmem = pl.BlockSpec(memory_space=pltpu.VMEM)
    hbm = pl.BlockSpec(memory_space=pl.ANY)
    outs = pl.pallas_call(
        functools.partial(kernel, n_seq, n_val),
        out_shape=(
            jax.ShapeDtypeStruct(values.shape, BF16),
            jax.ShapeDtypeStruct(queries.shape, F32),
            jax.ShapeDtypeStruct(keys.shape, F32),
            jax.ShapeDtypeStruct(values.shape, BF16),
        ),
        in_specs=[hbm, hbm, hbm, hbm],
        out_specs=(hbm, vmem, vmem, hbm),
        scratch_shapes=scratch,
        compiler_params=pltpu.CompilerParams(
            collective_id=0, has_side_effects=True, vmem_limit_bytes=56 << 20
        ),
        name="based_layer",
    )(queries, keys, values, out_grad)
    return pl.pallas_call(
        hand_on,
        out_shape=tuple(jax.ShapeDtypeStruct(o.shape, o.dtype) for o in outs),
        in_specs=[hbm] * len(outs),
        out_specs=(hbm,) * len(outs),
        scratch_shapes=[*[vm(o.shape, o.dtype) for o in outs], dma((2, len(outs)))],
        name="hand_on",
    )(*outs)


def solution(mesh):
    in_specs = (
        P("val", None, "seq"),
        P("val", None, "seq"),
        P(None, "val", "seq"),
        P(None, "val", "seq"),
    )
    out_specs = (
        P(None, "val", "seq"),
        P("val", None, "seq"),
        P("val", None, "seq"),
        P(None, "val", "seq"),
    )
    return jax.shard_map(local, mesh=mesh, in_specs=in_specs, out_specs=out_specs, check_vma=False)
```
